32 devices in a mesh: dp: 16 (over z, y, x), tensor: 2 (over core).
Axes of the slice: x: 2, y: 2, z: 4, core: 2. Of those that a mesh axis runs over, the one named last changes fastest.
Arguments:
- activations: bfloat16 [128, 577, 1024], P('dp'), may hold values from -6 to 6
- ln1_gain: bfloat16 [1024], replicated, may hold values from 0.099609375 to 1.8984375
- ln1_bias: bfloat16 [1024], replicated, may hold values from -2 to 2
- w_qkv: bfloat16 [3, 1024, 1024], P(None, None, 'tensor'), may hold values from -0.1875 to 0.1875
- qv_bias: bfloat16 [2, 1024], P(None, 'tensor'), may hold values from -3 to 3
- w_out: bfloat16 [1024, 1024], P('tensor'), may hold values from -2 to 2
- out_bias: bfloat16 [1024], replicated, may hold values from -2 to 2
- ln2_gain: bfloat16 [1024], replicated, may hold values from 0.099609375 to 1.8984375
- ln2_bias: bfloat16 [1024], replicated, may hold values from -2 to 2
- w_up: bfloat16 [1024, 4096], P(None, 'tensor'), may hold values from -0.1875 to 0.1875
- up_bias: bfloat16 [4096], P('tensor'), may hold values from -3 to 3
- w_down: bfloat16 [4096, 1024], P('tensor'), may hold values from -0.09375 to 0.09375
- down_bias: bfloat16 [1024], replicated, may hold values from -2 to 2
- cotangent: bfloat16 [128, 577, 1024], P('dp'), may hold values from -6 to 6
Outputs:
- layer_out: bfloat16 [128, 577, 1024], P(('dp', 'tensor'))
- grad_input: bfloat16 [128, 577, 1024], P(('dp', 'tensor'))
- grad_ln1_gain: float32 [1024], replicated
- grad_ln1_bias: float32 [1024], replicated
- grad_w_qkv: float32 [3, 1024, 1024], P(None, None, 'tensor')
- grad_qv_bias: float32 [2, 1024], P(None, 'tensor')
- grad_w_out: float32 [1024, 1024], P('tensor')
- grad_out_bias: float32 [1024], replicated
- grad_ln2_gain: float32 [1024], replicated
- grad_ln2_bias: float32 [1024], replicated
- grad_w_up: float32 [1024, 4096], P(None, 'tensor')
- grad_up_bias: float32 [4096], P('tensor')
- grad_w_down: float32 [4096, 1024], P('tensor')
- grad_down_bias: float32 [1024], replicated
The draws below stay inside these ranges and needn't reach their ends.
All inputs are finite; a program needn't handle non-finite values.
Results may differ from the reference program's by a relative error of at most 0.019.
Values may be sent and summed in bfloat16 or wider, within the bound.
No kernel may reach another device: no remote copies, remote signals or barrier semaphores. Data moves between devices by JAX's collectives and lax.ppermute only.
A program may use at most 448 MiB of HBM per device.

```python
import jax
import jax.numpy as jnp
from jax import lax

D = 1024
HEADS = 16
HEAD = 64
FF = 4096
SEQ = 577
IMAGES = 128


def steps_of(key, extent, cuts, smallest, largest):
    gain = 1.0
    for dim, shards_of in cuts:
        draws = jax.random.uniform(jax.random.fold_in(jax.random.fold_in(key, 6), dim), (shards_of,), jnp.float32, smallest / len(cuts), largest / len(cuts))
        gain = gain * jnp.repeat(jnp.exp(draws), extent[dim] // shards_of).reshape((-1,) + (1,) * (len(extent) - 1 - dim))
    return gain


def noise(stream_key, extent, width, reach, split=(), held_as=jnp.bfloat16):
    values = jax.random.normal(stream_key, extent, jnp.float32) * width
    if len(split) > 0:
        values = steps_of(stream_key, extent, split, -0.22, 0.18) * values
    return jnp.clip(values, min=-reach, max=reach).astype(held_as)


def setup_inputs(seed: int = 0) -> dict:
    seeds = jax.random.split(jax.random.key(seed), 15)
    activations = noise(seeds[0], (IMAGES, SEQ, D), 1.0, 6.0, ((0, 16),))
    ln1_gain = jnp.clip(1.0 + 0.18 * jax.random.normal(seeds[1], (D,), jnp.float32), 0.099609375, 1.8984375).astype(jnp.bfloat16)
    ln1_bias = noise(seeds[2], (D,), 0.3, 2.0)
    w_qkv = noise(seeds[3], (3, D, D), D ** -0.5, 0.1875, ((2, 2),))
    qv_bias = noise(seeds[4], (2, D), 0.5, 3.0, ((1, 2),))
    w_out = noise(seeds[5], (D, D), (4 * D // SEQ) ** -0.5, 2.0, ((0, 2),))
    out_bias = noise(seeds[6], (D,), 0.3, 2.0)
    ln2_gain = jnp.clip(1.0 + 0.18 * jax.random.normal(seeds[7], (D,), jnp.float32), 0.099609375, 1.8984375).astype(jnp.bfloat16)
    ln2_bias = noise(seeds[8], (D,), 0.3, 2.0)
    w_up = noise(seeds[9], (D, FF), D ** -0.5, 0.1875, ((1, 2),))
    up_bias = noise(seeds[10], (FF,), 0.5, 3.0, ((0, 2),))
    w_down = noise(seeds[11], (FF, D), FF ** -0.5, 0.09375, ((0, 2),))
    down_bias = noise(seeds[12], (D,), 0.3, 2.0)
    cotangent = noise(seeds[13], (IMAGES, SEQ, D), 1.0, 6.0, ((0, 16),))
    return {"activations": activations, "ln1_gain": ln1_gain, "ln1_bias": ln1_bias, "w_qkv": w_qkv, "qv_bias": qv_bias, "w_out": w_out, "out_bias": out_bias, "ln2_gain": ln2_gain, "ln2_bias": ln2_bias, "w_up": w_up, "up_bias": up_bias, "w_down": w_down, "down_bias": down_bias, "cotangent": cotangent}


EPSILON = 1e-06

@jax.custom_vjp
def low(v):
    return lax.optimization_barrier(v.astype(jnp.bfloat16)).astype(jnp.float32)

@jax.custom_vjp
def low_back(v):
    return v

def low_keep(v):
    return (low(v), None)

def low_pass(kept, grad):
    return (grad,)

def back_keep(v):
    return (v, None)

def back_low(kept, grad):
    return (low(grad),)
low.defvjp(low_keep, low_pass)
low_back.defvjp(back_keep, back_low)

def product(form, left, right):
    return jnp.einsum(form, left.astype(jnp.float32), right.astype(jnp.float32), precision=lax.Precision.HIGHEST)

def layer_norm(row_data, gain_vec, offset):
    center = row_data - lax.optimization_barrier(jnp.mean(row_data, axis=-1, keepdims=True))
    variance = lax.optimization_barrier(jnp.mean(center * center, axis=-1, keepdims=True))
    return center * lax.rsqrt(variance + EPSILON) * gain_vec + offset

def layer(inputs, gain_in, bias_in, w_qkv, qv_bias, w_out, out_bias, gain_mid, bias_mid, w_up, up_bias, w_down, down_bias):
    group = inputs.shape[0]
    normed_in = low(layer_norm(inputs, gain_in, bias_in))
    queries = low(low_back(product('gsd,de->gse', normed_in, w_qkv[0]) + qv_bias[0]))
    keys = low(low_back(product('gsd,de->gse', normed_in, w_qkv[1])))
    values = low(low_back(product('gsd,de->gse', normed_in, w_qkv[2]) + qv_bias[1]))
    shape = (group, SEQ, HEADS, HEAD)
    scores = low_back(product('gqhd,gkhd->ghqk', queries.reshape(shape), keys.reshape(shape)) * HEAD ** (-0.5))
    attn_probs = jax.nn.softmax(scores, axis=-1)
    mixed = product('ghqk,gkhd->gqhd', low(attn_probs), values.reshape(shape)).reshape(group, SEQ, D)
    mixed_heads = low(low_back(mixed))
    attention = low_back(product('gse,ed->gsd', mixed_heads, w_out))
    residual = inputs + attention + out_bias
    normed_mid = low(layer_norm(residual, gain_mid, bias_mid))
    hidden_pre = low_back(product('gsd,df->gsf', normed_mid, w_up) + up_bias)
    active = low(jax.nn.gelu(hidden_pre, approximate=False))
    feed_out = low_back(product('gsf,fd->gsd', active, w_down))
    return residual + feed_out + down_bias

def reference(activations, ln1_gain, ln1_bias, w_qkv, qv_bias, w_out, out_bias, ln2_gain, ln2_bias, w_up, up_bias, w_down, down_bias, cotangent):
    params = tuple((p.astype(jnp.float32) for p in (ln1_gain, ln1_bias, w_qkv, qv_bias, w_out, out_bias, ln2_gain, ln2_bias, w_up, up_bias, w_down, down_bias)))
    group = 4
    inputs_all = activations.astype(jnp.float32).reshape(-1, group, SEQ, D)
    cots_all = cotangent.astype(jnp.float32).reshape(-1, group, SEQ, D)

    def step(carry, pair):
        inputs, cots = pair
        result, pull = jax.vjp(layer, inputs, *params)
        grads = pull(cots)
        carry = tuple((c + g for c, g in zip(carry, grads[1:])))
        return (carry, (result.astype(jnp.bfloat16), grads[0].astype(jnp.bfloat16)))
    start = tuple((jnp.zeros_like(p) for p in params))
    totals, (outputs, grad_inputs) = lax.scan(step, start, (inputs_all, cots_all))
    return (outputs.reshape(IMAGES, SEQ, D), grad_inputs.reshape(IMAGES, SEQ, D), totals[0], totals[1], totals[2], totals[3], totals[4], totals[5], totals[6], totals[7], totals[8], totals[9], totals[10], totals[11])
```

```python
import functools

import jax
import jax.numpy as jnp
from jax import lax
from jax.experimental import pallas as pl
from jax.experimental.pallas import tpu as pltpu
from jax.sharding import PartitionSpec as P

HEAD = 64
PAIR = 2 * HEAD
EPSILON = 1e-06
ROOT_HALF = 0.7071067811865476
INV_ROOT_TWO_PI = 0.3989422804014327
MASKED = -1e30
BF16 = jnp.bfloat16
F32 = jnp.float32
VMEM_BYTES = 63 * 1024 * 1024
NT = (((1,), (1,)), ((), ()))
TN = (((0,), (0,)), ((), ()))


def up_to(count, step):
    return -(-count // step) * step


def cost(flops, moved):
    return pl.CostEstimate(flops=int(flops), bytes_accessed=int(moved), transcendentals=0)


def params(axes):
    return pltpu.CompilerParams(
        dimension_semantics=("arbitrary",) * axes, vmem_limit_bytes=VMEM_BYTES
    )


def norm_rows(rows, eps=EPSILON):
    center = rows - jnp.mean(rows, axis=-1, keepdims=True)
    inverse = lax.rsqrt(jnp.mean(center * center, axis=-1, keepdims=True) + eps)
    return center * inverse, inverse


def first_lanes():
    lane = lax.broadcasted_iota(jnp.int32, (1, PAIR), 1)
    return lane


def project_kernel(x_ref, gain_ref, bias_ref, w_ref, add_ref, normed_ref, out_ref):
    step = pl.program_id(1)
    rows = x_ref.shape[1]

    @pl.when(step == 0)
    def _():
        hat, _ = norm_rows(x_ref[0].astype(F32))
        normed_ref[...] = jnp.zeros_like(normed_ref)
        normed_ref[0:rows] = (hat * gain_ref[...] + bias_ref[...]).astype(BF16)

    scale = jnp.where(lax.rem(step, 3) == 0, HEAD ** (-0.5), 1.0).astype(F32)
    acc = jnp.dot(normed_ref[...], w_ref[0], preferred_element_type=F32) + add_ref[0]
    out_ref[0] = (acc * scale).astype(BF16)


def project(activations, gain, bias, w_all, add_all, share, padded):
    _, seq, width = activations.shape
    planes, _, columns = w_all.shape
    return pl.pallas_call(
        project_kernel,
        grid_spec=pl.GridSpec(
            grid=(share, planes),
            in_specs=[
                pl.BlockSpec((1, seq, width), lambda i, j: (i, 0, 0)),
                pl.BlockSpec((1, width), lambda i, j: (0, 0)),
                pl.BlockSpec((1, width), lambda i, j: (0, 0)),
                pl.BlockSpec((1, width, columns), lambda i, j: (j, 0, 0)),
                pl.BlockSpec((1, 1, columns), lambda i, j: (j, 0, 0)),
            ],
            out_specs=[
                pl.BlockSpec((padded, width), lambda i, j: (i, 0)),
                pl.BlockSpec((1, padded, columns), lambda i, j: (j, i, 0)),
            ],
        ),
        out_shape=[
            jax.ShapeDtypeStruct((share * padded, width), BF16),
            jax.ShapeDtypeStruct((planes, share * padded, columns), BF16),
        ],
        cost_estimate=cost(share * planes * 2 * padded * width * columns * 1.5, share * planes * 2e6),
        compiler_params=params(2),
        name="project",
    )(activations, gain, bias, w_all, add_all)


def attend_kernel(seq, keys_padded, q_ref, k_ref, v_ref, mixed_ref, inverse_ref, raised_ref):
    rows = q_ref.shape[1]
    lane = lax.broadcasted_iota(jnp.int32, (1, PAIR), 1)
    q = q_ref[0]
    extra = jnp.zeros((keys_padded - rows, PAIR), BF16)
    k = jnp.concatenate([k_ref[0], extra], axis=0)
    v = jnp.concatenate([v_ref[0], extra], axis=0)
    vx = jnp.concatenate([v, jnp.ones((keys_padded, PAIR), BF16)], axis=1)
    row = lax.broadcasted_iota(jnp.int32, (keys_padded, PAIR), 0)
    lane_k = lax.broadcasted_iota(jnp.int32, (keys_padded, PAIR), 1)
    lane_q = lax.broadcasted_iota(jnp.int32, (rows, PAIR), 1)
    results = []
    for head in range(2):
        mark = HEAD * (1 - head)
        inside_k = (lane_k // HEAD) == head
        inside_q = (lane_q // HEAD) == head
        hide = jnp.where((lane_k == mark) & (row >= seq), MASKED, 0.0).astype(BF16)
        one = jnp.where(lane_q == mark, 1.0, 0.0).astype(BF16)
        kx = jnp.where(inside_k, k, hide)
        qx = jnp.where(inside_q, q, one)
        scores = lax.dot_general(qx, kx, NT, preferred_element_type=F32)
        raised = jnp.exp(scores - jnp.max(scores, axis=-1, keepdims=True)).astype(BF16)
        raised_ref[0, head] = raised
        results.append(jnp.dot(raised, vx, preferred_element_type=F32))
    inside = (lane // HEAD) == 0
    total = jnp.where(inside, results[0][:, :PAIR], results[1][:, :PAIR])
    inverse = 1.0 / jnp.where(inside, results[0][:, PAIR:], results[1][:, PAIR:])
    mixed_ref[...] = (total * inverse).astype(BF16)
    inverse_ref[...] = inverse


def attend(qkv, share, padded, seq):
    planes, _, columns = qkv.shape
    per = columns // PAIR
    pairs = planes // 3 * per
    keys_padded = up_to(padded, 128)

    def plane(c):
        return lambda i, p: (p // per * 3 + c, i, p % per)

    return pl.pallas_call(
        functools.partial(attend_kernel, seq, keys_padded),
        grid=(share, pairs),
        in_specs=[pl.BlockSpec((1, padded, PAIR), plane(c)) for c in range(3)],
        out_specs=[
            pl.BlockSpec((padded, PAIR), lambda i, p: (i, p)),
            pl.BlockSpec((padded, PAIR), lambda i, p: (i, p)),
            pl.BlockSpec((1, 2, padded, keys_padded), lambda i, p: (i * pairs + p, 0, 0, 0)),
        ],
        out_shape=[
            jax.ShapeDtypeStruct((share * padded, pairs * PAIR), BF16),
            jax.ShapeDtypeStruct((share * padded, pairs * PAIR), F32),
            jax.ShapeDtypeStruct((share * pairs, 2, padded, keys_padded), BF16),
        ],
        cost_estimate=cost(share * pairs * 1e9, share * pairs * 3e6),
        compiler_params=params(2),
        name="attend",
    )(qkv, qkv, qkv)


def attend_back_kernel(
    keys_padded, q_ref, k_ref, v_ref, mixed_ref, inverse_ref, raised_ref, up_ref, out_ref
):
    rows = q_ref.shape[1]
    lane = lax.broadcasted_iota(jnp.int32, (1, PAIR), 1)
    lane_k = lax.broadcasted_iota(jnp.int32, (keys_padded, PAIR), 1)
    lane_q = lax.broadcasted_iota(jnp.int32, (rows, PAIR), 1)
    q = q_ref[0]
    extra = jnp.zeros((keys_padded - rows, PAIR), BF16)
    k = jnp.concatenate([k_ref[0], extra], axis=0)
    v = jnp.concatenate([v_ref[0], extra], axis=0)
    up_f = up_ref[...].astype(F32) * inverse_ref[...]
    up = up_f.astype(BF16)
    spread = pltpu.roll(-(up_f * mixed_ref[...].astype(F32)), HEAD, 1).astype(BF16)
    none = jnp.zeros_like(k)
    grad_q = None
    grad_k, grad_v = [], []
    for head in range(2):
        inside_k = (lane_k // HEAD) == head
        inside_q = (lane_q // HEAD) == head
        left = jnp.where(inside_q, up, spread)
        right = jnp.where(inside_k, v, jnp.ones_like(v))
        raised = raised_ref[0, head]
        shifted = lax.dot_general(left, right, NT, preferred_element_type=F32)
        grad_scores = (raised.astype(F32) * shifted).astype(BF16)
        part = jnp.dot(grad_scores, jnp.where(inside_k, k, none), preferred_element_type=F32)
        grad_q = part if grad_q is None else grad_q + part
        grad_k.append(lax.dot_general(grad_scores, q, TN, preferred_element_type=F32))
        grad_v.append(lax.dot_general(raised, up, TN, preferred_element_type=F32))
    inside = (lane // HEAD) == 0
    out_ref[0, 0] = (grad_q * HEAD ** (-0.5)).astype(BF16)
    out_ref[0, 1] = jnp.where(inside, grad_k[0], grad_k[1])[:rows].astype(BF16)
    out_ref[0, 2] = jnp.where(inside, grad_v[0], grad_v[1])[:rows].astype(BF16)


def attend_back(qkv, mixed, inverse, raised, upstream, share, padded, first, count, into):
    planes, tokens, columns = qkv.shape
    per = columns // PAIR
    pairs = planes // 3 * per
    keys_padded = up_to(padded, 128)

    def plane(c):
        return lambda i, p: (p // per * 3 + c, first + i, p % per)

    column = pl.BlockSpec((padded, PAIR), lambda i, p: (first + i, p))
    operands = [qkv, qkv, qkv, mixed, inverse, raised, upstream]
    in_specs = [pl.BlockSpec((1, padded, PAIR), plane(c)) for c in range(3)] + [
        column,
        column,
        pl.BlockSpec(
            (1, 2, padded, keys_padded), lambda i, p: ((first + i) * pairs + p, 0, 0, 0)
        ),
        column,
    ]
    aliases = {}
    if into is not None:
        aliases = {len(operands): 0}
        operands.append(into)
        in_specs.append(pl.BlockSpec(memory_space=pl.ANY))

    def kernel(*refs):
        attend_back_kernel(keys_padded, *refs[:7], refs[-1])

    return pl.pallas_call(
        kernel,
        grid=(count, pairs),
        in_specs=in_specs,
        out_specs=pl.BlockSpec(
            (1, 3, padded, PAIR), lambda i, p: (p // per, 0, first + i, p % per)
        ),
        out_shape=jax.ShapeDtypeStruct((planes // 3, 3, tokens, columns), BF16),
        input_output_aliases=aliases,
        compiler_params=params(2),
        cost_estimate=cost(count * pairs * 1.1e9, count * pairs * 3e6),
        name="attend_back",
    )(*operands)


def middle_kernel(
    x_ref, cot_ref, mixed_ref, w_ref, add_ref, gain_ref, bias_ref, res_ref, normed_ref, cotp_ref
):
    rows = x_ref.shape[1]
    res_ref[...] = jnp.dot(mixed_ref[...], w_ref[...], preferred_element_type=F32) + add_ref[...]
    res_ref[0:rows] += x_ref[0].astype(F32)
    hat, _ = norm_rows(res_ref[...])
    normed_ref[...] = (hat * gain_ref[...] + bias_ref[...]).astype(BF16)
    cotp_ref[...] = jnp.zeros_like(cotp_ref)
    cotp_ref[0:rows] = cot_ref[0]


def middle(activations, cotangent, mixed, w_out, add, gain, bias, share, padded):
    _, seq, width = activations.shape
    vector = pl.BlockSpec((1, width), lambda i: (0, 0))
    image = pl.BlockSpec((1, seq, width), lambda i: (i, 0, 0))
    rows = pl.BlockSpec((padded, width), lambda i: (i, 0))
    tokens = share * padded
    return pl.pallas_call(
        middle_kernel,
        grid_spec=pl.GridSpec(
            grid=(share,),
            in_specs=[
                image,
                image,
                pl.BlockSpec((padded, mixed.shape[1]), lambda i: (i, 0)),
                pl.BlockSpec(w_out.shape, lambda i: (0, 0)),
                vector,
                vector,
                vector,
            ],
            out_specs=[rows, rows, rows],
        ),
        out_shape=[
            jax.ShapeDtypeStruct((tokens, width), F32),
            jax.ShapeDtypeStruct((tokens, width), BF16),
            jax.ShapeDtypeStruct((tokens, width), BF16),
        ],
        cost_estimate=cost(tokens * width * width * 6, tokens * width * 14),
        compiler_params=params(1),
        name="middle",
    )(activations, cotangent, mixed, w_out, add, gain, bias)


def feed_kernel(
    normed_ref,
    cot_ref,
    res_ref,
    wu_ref,
    wd_ref,
    ub_ref,
    db_ref,
    gain_ref,
    wo_ref,
    active_ref,
    pre_ref,
    out_ref,
    branch_ref,
    mixed_ref,
    ubsum_ref,
    sums_ref,
    feed_acc,
    normed_acc,
):
    step = pl.program_id(1)
    rows = out_ref.shape[1]
    wu = wu_ref[0]
    wd = wd_ref[...]
    hidden = jnp.dot(normed_ref[...], wu, preferred_element_type=F32) + ub_ref[...]
    back = lax.dot_general(cot_ref[...], wd, NT, preferred_element_type=F32)
    below = 0.5 * (1.0 + lax.erf(hidden * ROOT_HALF))
    slope = below + hidden * (INV_ROOT_TWO_PI * jnp.exp(-0.5 * hidden * hidden))
    active = (hidden * below).astype(BF16)
    pre_f = back * slope
    pre = pre_f.astype(BF16)
    active_ref[...] = active
    pre_ref[0] = pre
    ubsum_ref[0] = jnp.broadcast_to(jnp.sum(pre_f, axis=0, keepdims=True), ubsum_ref.shape[1:])
    feed = jnp.dot(active, wd, preferred_element_type=F32)
    normed = lax.dot_general(pre, wu, NT, preferred_element_type=F32)

    @pl.when(step == 0)
    def _():
        feed_acc[...] = feed
        normed_acc[...] = normed

    @pl.when(step > 0)
    def _():
        feed_acc[...] += feed
        normed_acc[...] += normed

    @pl.when(step == pl.num_programs(1) - 1)
    def _():
        res = res_ref[...]
        out_ref[0] = (res + feed_acc[...] + db_ref[...])[0:rows].astype(BF16)
        hat, inverse = norm_rows(res)
        grad = normed_acc[...]
        scaled = grad * gain_ref[...]
        cot = cot_ref[...].astype(F32)
        total = cot + inverse * (
            scaled
            - jnp.mean(scaled, axis=-1, keepdims=True)
            - hat * jnp.mean(scaled * hat, axis=-1, keepdims=True)
        )
        branch = total.astype(BF16)
        branch_ref[...] = branch
        mixed_ref[...] = lax.dot_general(branch, wo_ref[...], NT, preferred_element_type=F32).astype(BF16)
        sums_ref[0, 0:1] = jnp.sum(grad * hat, axis=0, keepdims=True)
        sums_ref[0, 1:2] = jnp.sum(grad, axis=0, keepdims=True)
        sums_ref[0, 2:3] = jnp.sum(total, axis=0, keepdims=True)
        sums_ref[0, 3:4] = jnp.sum(cot, axis=0, keepdims=True)
        sums_ref[0, 4:8] = jnp.zeros((4, sums_ref.shape[2]), F32)


def feed(normed, cot, res, w_up, w_down, up_bias, down_bias, gain, w_out, share, padded, seq):
    group, width, local = w_up.shape
    hidden = group * local
    block = min(512, local)
    per = local // block
    tokens = share * padded
    rows = pl.BlockSpec((padded, width), lambda i, f: (i, 0))
    vector = pl.BlockSpec((1, width), lambda i, f: (0, 0))
    return pl.pallas_call(
        feed_kernel,
        grid=(share, hidden // block),
        in_specs=[
            rows,
            rows,
            rows,
            pl.BlockSpec((1, width, block), lambda i, f: (f // per, 0, f % per)),
            pl.BlockSpec((block, width), lambda i, f: (f, 0)),
            pl.BlockSpec((1, block), lambda i, f: (0, f)),
            vector,
            vector,
            pl.BlockSpec(w_out.shape, lambda i, f: (0, 0)),
        ],
        out_specs=[
            pl.BlockSpec((padded, block), lambda i, f: (i, f)),
            pl.BlockSpec((1, padded, block), lambda i, f: (f // per, i, f % per)),
            pl.BlockSpec((1, seq, width), lambda i, f: (i, 0, 0)),
            rows,
            rows,
            pl.BlockSpec((1, 8, block), lambda i, f: (i, 0, f)),
            pl.BlockSpec((1, 8, width), lambda i, f: (i, 0, 0)),
        ],
        out_shape=[
            jax.ShapeDtypeStruct((tokens, hidden), BF16),
            jax.ShapeDtypeStruct((group, tokens, local), BF16),
            jax.ShapeDtypeStruct((share, seq, width), BF16),
            jax.ShapeDtypeStruct((tokens, width), BF16),
            jax.ShapeDtypeStruct((tokens, w_out.shape[0]), BF16),
            jax.ShapeDtypeStruct((share, 8, hidden), F32),
            jax.ShapeDtypeStruct((share, 8, width), F32),
        ],
        scratch_shapes=[pltpu.VMEM((padded, width), F32), pltpu.VMEM((padded, width), F32)],
        cost_estimate=cost(8 * tokens * width * hidden * 1.4, share * 3e7),
        compiler_params=params(2),
        name="feed",
    )(normed, cot, res, w_up, w_down, up_bias, down_bias, gain, w_out)


def input_kernel(x_ref, grad_ref, w_ref, branch_ref, gain_ref, out_ref, qsum_ref, sums_ref, acc):
    step = pl.program_id(1)
    rows = x_ref.shape[1]
    grad = grad_ref[0]
    part = lax.dot_general(grad, w_ref[0], NT, preferred_element_type=F32)
    qsum_ref[0, 0] = jnp.broadcast_to(
        jnp.sum(grad.astype(F32), axis=0, keepdims=True), qsum_ref.shape[2:]
    )

    @pl.when(step == 0)
    def _():
        acc[...] = part

    @pl.when(step > 0)
    def _():
        acc[...] += part

    @pl.when(step == pl.num_programs(1) - 1)
    def _():
        hat, inverse = norm_rows(x_ref[0].astype(F32))
        normed = acc[0:rows]
        scaled = normed * gain_ref[...]
        out_ref[0] = (
            branch_ref[0:rows].astype(F32)
            + inverse
            * (
                scaled
                - jnp.mean(scaled, axis=-1, keepdims=True)
                - hat * jnp.mean(scaled * hat, axis=-1, keepdims=True)
            )
        ).astype(BF16)
        sums_ref[0, 0:1] = jnp.sum(normed * hat, axis=0, keepdims=True)
        sums_ref[0, 1:2] = jnp.sum(normed, axis=0, keepdims=True)
        sums_ref[0, 2:8] = jnp.zeros((6, sums_ref.shape[2]), F32)


def input_back(activations, grads, w_all, branch, gain, share, padded):
    _, seq, width = activations.shape
    planes, _, columns = w_all.shape
    return pl.pallas_call(
        input_kernel,
        grid_spec=pl.GridSpec(
            grid=(share, planes),
            in_specs=[
                pl.BlockSpec((1, seq, width), lambda i, j: (i, 0, 0)),
                pl.BlockSpec((1, padded, columns), lambda i, j: (j, i, 0)),
                pl.BlockSpec((1, width, columns), lambda i, j: (j, 0, 0)),
                pl.BlockSpec((padded, width), lambda i, j: (i, 0)),
                pl.BlockSpec((1, width), lambda i, j: (0, 0)),
            ],
            out_specs=[
                pl.BlockSpec((1, seq, width), lambda i, j: (i, 0, 0)),
                pl.BlockSpec((1, 1, 8, columns), lambda i, j: (i, j, 0, 0)),
                pl.BlockSpec((1, 8, width), lambda i, j: (i, 0, 0)),
            ],
            scratch_shapes=[pltpu.VMEM((padded, width), F32)],
        ),
        out_shape=[
            jax.ShapeDtypeStruct((share, seq, width), BF16),
            jax.ShapeDtypeStruct((share, planes, 8, columns), F32),
            jax.ShapeDtypeStruct((share, 8, width), F32),
        ],
        compiler_params=params(2),
        cost_estimate=cost(share * planes * 2 * padded * width * columns * 2, share * planes * 3e6),
        name="input_back",
    )(activations, grads, w_all, branch, gain)


def swapped(value, axis, mask):
    size = lax.axis_size(axis)
    return lax.ppermute(value, axis, [(i, i ^ mask) for i in range(size)])


def spread_parts(value):
    size = lax.axis_size("tensor")
    return [value] + [swapped(value, "tensor", r) for r in range(1, size)]


def pair_sum(values):
    while len(values) > 1:
        values = [values[i] + values[i + 1] for i in range(0, len(values), 2)]
    return values[0]


def phases():
    size = lax.axis_size("dp")
    found, stride = [], 1
    while stride < size:
        span = min(4, size // stride)
        found.append((stride, span))
        stride *= span
    return found


def place(stride, span):
    return lax.rem(lax.div(lax.axis_index("dp"), stride), span)


def scatter_phase(value, stride, span):
    rows = value.shape[0] // span
    mine = place(stride, span)

    def piece(r):
        return lax.dynamic_slice_in_dim(value, (mine ^ r) * rows, rows, 0)

    terms = [piece(0)] + [swapped(piece(r), "dp", r * stride) for r in range(1, span)]
    return pair_sum([t.astype(F32) for t in terms]).astype(BF16)


def gather_phase(value, stride, span, into, offset):
    rows = value.shape[0]
    mine = place(stride, span)
    for r in range(span):
        got = value if r == 0 else swapped(value, "dp", r * stride)
        into = lax.dynamic_update_slice_in_dim(
            into, got.astype(into.dtype), offset + (mine ^ r) * rows, 0
        )
    return into


def tensor_sum(parts):
    terms = [parts[0]] + [swapped(parts[r], "tensor", r) for r in range(1, len(parts))]
    return pair_sum([t.astype(F32) for t in terms]).astype(BF16)


def weight_sum(value):
    order = phases()
    rows, columns = value.shape
    first = rows * 3 // 4
    colours = [(0, first, order), (first, rows - first, order[::-1])]
    out = jnp.zeros((rows, columns), F32)
    for offset, count, steps in colours:
        held = value[offset : offset + count]
        for stride, span in steps:
            held = scatter_phase(held, stride, span)
        for stride, span in steps[:0:-1]:
            held = gather_phase(
                held, stride, span, jnp.zeros((held.shape[0] * span, columns), BF16), 0
            )
        stride, span = steps[0]
        out = gather_phase(held, stride, span, out, offset)
    return out


def after(value, *earlier):
    return lax.optimization_barrier((value,) + earlier)[0]


def per_device(
    activations,
    ln1_gain,
    ln1_bias,
    w_qkv,
    qv_bias,
    w_out,
    out_bias,
    ln2_gain,
    ln2_bias,
    w_up,
    up_bias,
    w_down,
    down_bias,
    cotangent,
):
    group = lax.axis_size("tensor")
    position = lax.axis_index("tensor")
    images, seq, width = activations.shape
    share = images // group
    padded = up_to(seq, 16)
    columns = w_qkv.shape[2]
    local = w_up.shape[1]

    def row(vector):
        return vector.astype(F32).reshape(1, -1)

    inputs = lax.dynamic_slice_in_dim(activations, position * share, share, 0)
    cot_share = lax.dynamic_slice_in_dim(cotangent, position * share, share, 0)
    wqkv_all = jnp.concatenate(spread_parts(w_qkv), axis=0)
    small_all = jnp.stack(spread_parts(jnp.concatenate([qv_bias.reshape(-1), up_bias])))
    wout_all = jnp.concatenate(spread_parts(w_out), axis=0)
    wup_all = jnp.stack(spread_parts(w_up))
    wdown_all = jnp.concatenate(spread_parts(w_down), axis=0)

    qv_all = small_all[:, : 2 * columns].reshape(group, 2, columns).astype(F32)
    up_all = small_all[:, 2 * columns :].reshape(1, group * local).astype(F32)
    add_all = jnp.stack([qv_all[:, 0], jnp.zeros_like(qv_all[:, 0]), qv_all[:, 1]], axis=1).reshape(
        group * 3, 1, columns
    )

    normed_in, qkv = project(
        inputs, row(ln1_gain), row(ln1_bias), wqkv_all, add_all, share, padded
    )
    mixed, inverse, raised = attend(qkv, share, padded, seq)
    res, normed_mid, cot = middle(
        inputs, cot_share, mixed, wout_all, row(out_bias), row(ln2_gain), row(ln2_bias),
        share, padded,
    )
    active, pre, layer_out, branch, grad_mixed, up_sums, mid_sums = feed(
        normed_mid, cot, res, wup_all, wdown_all, up_all, row(down_bias), row(ln2_gain), wout_all,
        share, padded, seq,
    )
    down = lax.dot_general(active, cot, TN, preferred_element_type=F32).astype(BF16)
    pre = after(pre, down)
    up = [
        lax.dot_general(normed_mid, pre[r], TN, preferred_element_type=F32).astype(BF16)
        for r in range(group)
    ]
    branch_w = after(branch, *up)
    out = lax.dot_general(mixed, branch_w, TN, preferred_element_type=F32).astype(BF16)
    down = tensor_sum([down[r * local : (r + 1) * local] for r in range(group)])
    up = tensor_sum(up)
    out = tensor_sum([out[r * columns : (r + 1) * columns] for r in range(group)])
    grad_mixed = after(grad_mixed, down, up, out)
    grad_w_down, grad_w_up, grad_w_out = (
        g.astype(F32) for g in lax.psum((down, up, out), "dp")
    )
    grads = None
    for image in range(share):
        grads = attend_back(
            qkv, mixed, inverse, raised, grad_mixed, share, padded, image, 1, grads
        )
    in_planes = grads.reshape(qkv.shape)
    heads_w = [
        jnp.einsum("cte,td->ced", grads[r], normed_in, preferred_element_type=F32)
        .astype(BF16)
        .reshape(3 * columns, width)
        for r in range(group)
    ]
    heads_w = tensor_sum(heads_w)
    in_planes = after(in_planes, heads_w)
    grad_w_qkv = weight_sum(heads_w).reshape(3, columns, width).swapaxes(1, 2)
    grad_input, qkv_sums, in_sums = input_back(
        inputs, in_planes, wqkv_all, branch, row(ln1_gain), share, padded
    )
    in_sum = jnp.sum(in_sums, axis=0)
    mid_sum = jnp.sum(mid_sums, axis=0)
    qkv_sum = jnp.sum(qkv_sums[:, :, 0], axis=0).reshape(group, 3, columns)
    up_sum = jnp.sum(up_sums[:, 0], axis=0).reshape(group, local)
    shards = jnp.concatenate([qkv_sum[:, 0], qkv_sum[:, 2], up_sum], axis=1)
    shard = pair_sum([shards[0]] + [swapped(shards[r], "tensor", r) for r in range(1, group)])
    whole = jnp.concatenate([in_sum[:2], mid_sum[:4]], axis=0)
    whole = pair_sum([whole] + [swapped(whole, "tensor", r) for r in range(1, group)])
    vectors = jnp.concatenate([whole.reshape(-1), shard])
    for stride, span in phases():
        vectors = pair_sum(
            [vectors] + [swapped(vectors, "dp", r * stride) for r in range(1, span)]
        )
    whole = vectors[: 6 * width].reshape(6, width)
    rest = vectors[6 * width :]
    grad_qv = rest[: 2 * columns].reshape(2, columns)
    grad_up_bias = rest[2 * columns :]
    return (
        layer_out,
        grad_input,
        whole[0],
        whole[1],
        grad_w_qkv,
        grad_qv,
        grad_w_out,
        whole[4],
        whole[2],
        whole[3],
        grad_w_up,
        grad_up_bias,
        grad_w_down,
        whole[5],
    )


def solution(mesh):
    placed = (
        P("dp", None, None),
        P(),
        P(),
        P(None, None, "tensor"),
        P(None, "tensor"),
        P("tensor", None),
        P(),
        P(),
        P(),
        P(None, "tensor"),
        P("tensor"),
        P("tensor", None),
        P(),
        P("dp", None, None),
    )
    return jax.shard_map(
        per_device,
        mesh=mesh,
        in_specs=placed,
        out_specs=(
            P(("dp", "tensor"), None, None),
            P(("dp", "tensor"), None, None),
            P(),
            P(),
            P(None, None, "tensor"),
            P(None, "tensor"),
            P("tensor", None),
            P(),
            P(),
            P(),
            P(None, "tensor"),
            P("tensor"),
            P("tensor", None),
            P(),
        ),
        check_vma=False,
    )
```

```python
import functools

import jax
import jax.numpy as jnp
from jax import lax
from jax.experimental import pallas as pl
from jax.experimental.pallas import tpu as pltpu
from jax.sharding import PartitionSpec as P

HEAD = 64
PAIR = 2 * HEAD
EPSILON = 1e-06
ROOT_HALF = 0.7071067811865476
INV_ROOT_TWO_PI = 0.3989422804014327
MASKED = -1e30
BF16 = jnp.bfloat16
F32 = jnp.float32
VMEM_BYTES = 63 * 1024 * 1024
NT = (((1,), (1,)), ((), ()))
TN = (((0,), (0,)), ((), ()))


def up_to(count, step):
    return -(-count // step) * step


def cost(flops, moved):
    return pl.CostEstimate(flops=int(flops), bytes_accessed=int(moved), transcendentals=0)


def params(axes):
    return pltpu.CompilerParams(
        dimension_semantics=("arbitrary",) * axes, vmem_limit_bytes=VMEM_BYTES
    )


def norm_rows(rows, eps=EPSILON):
    center = rows - jnp.mean(rows, axis=-1, keepdims=True)
    inverse = lax.rsqrt(jnp.mean(center * center, axis=-1, keepdims=True) + eps)
    return center * inverse, inverse


def first_lanes():
    lane = lax.broadcasted_iota(jnp.int32, (1, PAIR), 1)
    return lane


def project_kernel(x_ref, gain_ref, bias_ref, w_ref, add_ref, normed_ref, out_ref):
    step = pl.program_id(1)
    rows = x_ref.shape[1]

    @pl.when(step == 0)
    def _():
        hat, _ = norm_rows(x_ref[0].astype(F32))
        normed_ref[...] = jnp.zeros_like(normed_ref)
        normed_ref[0:rows] = (hat * gain_ref[...] + bias_ref[...]).astype(BF16)

    scale = jnp.where(lax.rem(step, 3) == 0, HEAD ** (-0.5), 1.0).astype(F32)
    acc = jnp.dot(normed_ref[...], w_ref[0], preferred_element_type=F32) + add_ref[0]
    out_ref[0] = (acc * scale).astype(BF16)


def project(activations, gain, bias, w_all, add_all, share, padded):
    _, seq, width = activations.shape
    planes, _, columns = w_all.shape
    return pl.pallas_call(
        project_kernel,
        grid_spec=pl.GridSpec(
            grid=(share, planes),
            in_specs=[
                pl.BlockSpec((1, seq, width), lambda i, j: (i, 0, 0)),
                pl.BlockSpec((1, width), lambda i, j: (0, 0)),
                pl.BlockSpec((1, width), lambda i, j: (0, 0)),
                pl.BlockSpec((1, width, columns), lambda i, j: (j, 0, 0)),
                pl.BlockSpec((1, 1, columns), lambda i, j: (j, 0, 0)),
            ],
            out_specs=[
                pl.BlockSpec((padded, width), lambda i, j: (i, 0)),
                pl.BlockSpec((1, padded, columns), lambda i, j: (j, i, 0)),
            ],
        ),
        out_shape=[
            jax.ShapeDtypeStruct((share * padded, width), BF16),
            jax.ShapeDtypeStruct((planes, share * padded, columns), BF16),
        ],
        cost_estimate=cost(share * planes * 2 * padded * width * columns * 1.5, share * planes * 2e6),
        compiler_params=params(2),
        name="project",
    )(activations, gain, bias, w_all, add_all)


def attend_kernel(seq, keys_padded, q_ref, k_ref, v_ref, mixed_ref, inverse_ref, raised_ref):
    rows = q_ref.shape[1]
    lane = lax.broadcasted_iota(jnp.int32, (1, PAIR), 1)
    q = q_ref[0]
    extra = jnp.zeros((keys_padded - rows, PAIR), BF16)
    k = jnp.concatenate([k_ref[0], extra], axis=0)
    v = jnp.concatenate([v_ref[0], extra], axis=0)
    vx = jnp.concatenate([v, jnp.ones((keys_padded, PAIR), BF16)], axis=1)
    row = lax.broadcasted_iota(jnp.int32, (keys_padded, PAIR), 0)
    lane_k = lax.broadcasted_iota(jnp.int32, (keys_padded, PAIR), 1)
    lane_q = lax.broadcasted_iota(jnp.int32, (rows, PAIR), 1)
    results = []
    for head in range(2):
        mark = HEAD * (1 - head)
        inside_k = (lane_k // HEAD) == head
        inside_q = (lane_q // HEAD) == head
        hide = jnp.where((lane_k == mark) & (row >= seq), MASKED, 0.0).astype(BF16)
        one = jnp.where(lane_q == mark, 1.0, 0.0).astype(BF16)
        kx = jnp.where(inside_k, k, hide)
        qx = jnp.where(inside_q, q, one)
        scores = lax.dot_general(qx, kx, NT, preferred_element_type=F32)
        raised = jnp.exp(scores - jnp.max(scores, axis=-1, keepdims=True)).astype(BF16)
        raised_ref[0, head] = raised
        results.append(jnp.dot(raised, vx, preferred_element_type=F32))
    inside = (lane // HEAD) == 0
    total = jnp.where(inside, results[0][:, :PAIR], results[1][:, :PAIR])
    inverse = 1.0 / jnp.where(inside, results[0][:, PAIR:], results[1][:, PAIR:])
    mixed_ref[...] = (total * inverse).astype(BF16)
    inverse_ref[...] = inverse


def attend(qkv, share, padded, seq):
    planes, _, columns = qkv.shape
    per = columns // PAIR
    pairs = planes // 3 * per
    keys_padded = up_to(padded, 128)

    def plane(c):
        return lambda i, p: (p // per * 3 + c, i, p % per)

    return pl.pallas_call(
        functools.partial(attend_kernel, seq, keys_padded),
        grid=(share, pairs),
        in_specs=[pl.BlockSpec((1, padded, PAIR), plane(c)) for c in range(3)],
        out_specs=[
            pl.BlockSpec((padded, PAIR), lambda i, p: (i, p)),
            pl.BlockSpec((padded, PAIR), lambda i, p: (i, p)),
            pl.BlockSpec((1, 2, padded, keys_padded), lambda i, p: (i * pairs + p, 0, 0, 0)),
        ],
        out_shape=[
            jax.ShapeDtypeStruct((share * padded, pairs * PAIR), BF16),
            jax.ShapeDtypeStruct((share * padded, pairs * PAIR), F32),
            jax.ShapeDtypeStruct((share * pairs, 2, padded, keys_padded), BF16),
        ],
        cost_estimate=cost(share * pairs * 1e9, share * pairs * 3e6),
        compiler_params=params(2),
        name="attend",
    )(qkv, qkv, qkv)


def attend_back_kernel(
    keys_padded, q_ref, k_ref, v_ref, mixed_ref, inverse_ref, raised_ref, up_ref, out_ref
):
    rows = q_ref.shape[1]
    lane = lax.broadcasted_iota(jnp.int32, (1, PAIR), 1)
    lane_k = lax.broadcasted_iota(jnp.int32, (keys_padded, PAIR), 1)
    lane_q = lax.broadcasted_iota(jnp.int32, (rows, PAIR), 1)
    q = q_ref[0]
    extra = jnp.zeros((keys_padded - rows, PAIR), BF16)
    k = jnp.concatenate([k_ref[0], extra], axis=0)
    v = jnp.concatenate([v_ref[0], extra], axis=0)
    up_f = up_ref[...].astype(F32) * inverse_ref[...]
    up = up_f.astype(BF16)
    spread = pltpu.roll(-(up_f * mixed_ref[...].astype(F32)), HEAD, 1).astype(BF16)
    none = jnp.zeros_like(k)
    grad_q = None
    grad_k, grad_v = [], []
    for head in range(2):
        inside_k = (lane_k // HEAD) == head
        inside_q = (lane_q // HEAD) == head
        left = jnp.where(inside_q, up, spread)
        right = jnp.where(inside_k, v, jnp.ones_like(v))
        raised = raised_ref[0, head]
        shifted = lax.dot_general(left, right, NT, preferred_element_type=F32)
        grad_scores = (raised.astype(F32) * shifted).astype(BF16)
        part = jnp.dot(grad_scores, jnp.where(inside_k, k, none), preferred_element_type=F32)
        grad_q = part if grad_q is None else grad_q + part
        grad_k.append(lax.dot_general(grad_scores, q, TN, preferred_element_type=F32))
        grad_v.append(lax.dot_general(raised, up, TN, preferred_element_type=F32))
    inside = (lane // HEAD) == 0
    out_ref[0, 0] = (grad_q * HEAD ** (-0.5)).astype(BF16)
    out_ref[0, 1] = jnp.where(inside, grad_k[0], grad_k[1])[:rows].astype(BF16)
    out_ref[0, 2] = jnp.where(inside, grad_v[0], grad_v[1])[:rows].astype(BF16)


def attend_back(qkv, mixed, inverse, raised, upstream, padded, first, pair0, count, into):
    planes, tokens, columns = qkv.shape
    per = columns // PAIR
    pairs = planes // 3 * per
    keys_padded = up_to(padded, 128)

    def plane(c):
        return lambda p: ((pair0 + p) // per * 3 + c, first, (pair0 + p) % per)

    column = pl.BlockSpec((padded, PAIR), lambda p: (first, pair0 + p))
    operands = [qkv, qkv, qkv, mixed, inverse, raised, upstream]
    in_specs = [pl.BlockSpec((1, padded, PAIR), plane(c)) for c in range(3)] + [
        column,
        column,
        pl.BlockSpec(
            (1, 2, padded, keys_padded), lambda p: (first * pairs + pair0 + p, 0, 0, 0)
        ),
        column,
    ]
    aliases = {}
    if into is not None:
        aliases = {len(operands): 0}
        operands.append(into)
        in_specs.append(pl.BlockSpec(memory_space=pl.ANY))

    def kernel(*refs):
        attend_back_kernel(keys_padded, *refs[:7], refs[-1])

    return pl.pallas_call(
        kernel,
        grid=(count,),
        in_specs=in_specs,
        out_specs=pl.BlockSpec(
            (1, 3, padded, PAIR), lambda p: ((pair0 + p) // per, 0, first, (pair0 + p) % per)
        ),
        out_shape=jax.ShapeDtypeStruct((planes // 3, 3, tokens, columns), BF16),
        input_output_aliases=aliases,
        compiler_params=params(1),
        cost_estimate=cost(count * 1.3e9, count * 3e6),
        name="attend_back",
    )(*operands)


def middle_kernel(
    x_ref, cot_ref, mixed_ref, w_ref, add_ref, gain_ref, bias_ref, res_ref, normed_ref, cotp_ref
):
    rows = x_ref.shape[1]
    res_ref[...] = jnp.dot(mixed_ref[...], w_ref[...], preferred_element_type=F32) + add_ref[...]
    res_ref[0:rows] += x_ref[0].astype(F32)
    hat, _ = norm_rows(res_ref[...])
    normed_ref[...] = (hat * gain_ref[...] + bias_ref[...]).astype(BF16)
    cotp_ref[...] = jnp.zeros_like(cotp_ref)
    cotp_ref[0:rows] = cot_ref[0]


def middle(activations, cotangent, mixed, w_out, add, gain, bias, share, padded):
    _, seq, width = activations.shape
    vector = pl.BlockSpec((1, width), lambda i: (0, 0))
    image = pl.BlockSpec((1, seq, width), lambda i: (i, 0, 0))
    rows = pl.BlockSpec((padded, width), lambda i: (i, 0))
    tokens = share * padded
    return pl.pallas_call(
        middle_kernel,
        grid_spec=pl.GridSpec(
            grid=(share,),
            in_specs=[
                image,
                image,
                pl.BlockSpec((padded, mixed.shape[1]), lambda i: (i, 0)),
                pl.BlockSpec(w_out.shape, lambda i: (0, 0)),
                vector,
                vector,
                vector,
            ],
            out_specs=[rows, rows, rows],
        ),
        out_shape=[
            jax.ShapeDtypeStruct((tokens, width), F32),
            jax.ShapeDtypeStruct((tokens, width), BF16),
            jax.ShapeDtypeStruct((tokens, width), BF16),
        ],
        cost_estimate=cost(tokens * width * width * 6, tokens * width * 14),
        compiler_params=params(1),
        name="middle",
    )(activations, cotangent, mixed, w_out, add, gain, bias)


def feed_kernel(
    normed_ref,
    cot_ref,
    res_ref,
    wu_ref,
    wd_ref,
    ub_ref,
    db_ref,
    gain_ref,
    wo_ref,
    active_ref,
    pre_ref,
    out_ref,
    branch_ref,
    mixed_ref,
    ubsum_ref,
    sums_ref,
    feed_acc,
    normed_acc,
):
    step = pl.program_id(1)
    rows = out_ref.shape[1]
    wu = wu_ref[0]
    wd = wd_ref[...]
    hidden = jnp.dot(normed_ref[...], wu, preferred_element_type=F32) + ub_ref[...]
    back = lax.dot_general(cot_ref[...], wd, NT, preferred_element_type=F32)
    below = 0.5 * (1.0 + lax.erf(hidden * ROOT_HALF))
    slope = below + hidden * (INV_ROOT_TWO_PI * jnp.exp(-0.5 * hidden * hidden))
    active = (hidden * below).astype(BF16)
    pre_f = back * slope
    pre = pre_f.astype(BF16)
    active_ref[...] = active
    pre_ref[0] = pre
    ubsum_ref[0] = jnp.broadcast_to(jnp.sum(pre_f, axis=0, keepdims=True), ubsum_ref.shape[1:])
    feed = jnp.dot(active, wd, preferred_element_type=F32)
    normed = lax.dot_general(pre, wu, NT, preferred_element_type=F32)

    @pl.when(step == 0)
    def _():
        feed_acc[...] = feed
        normed_acc[...] = normed

    @pl.when(step > 0)
    def _():
        feed_acc[...] += feed
        normed_acc[...] += normed

    @pl.when(step == pl.num_programs(1) - 1)
    def _():
        res = res_ref[...]
        out_ref[0] = (res + feed_acc[...] + db_ref[...])[0:rows].astype(BF16)
        hat, inverse = norm_rows(res)
        grad = normed_acc[...]
        scaled = grad * gain_ref[...]
        cot = cot_ref[...].astype(F32)
        total = cot + inverse * (
            scaled
            - jnp.mean(scaled, axis=-1, keepdims=True)
            - hat * jnp.mean(scaled * hat, axis=-1, keepdims=True)
        )
        branch = total.astype(BF16)
        branch_ref[...] = branch
        mixed_ref[...] = lax.dot_general(branch, wo_ref[...], NT, preferred_element_type=F32).astype(BF16)
        sums_ref[0, 0:1] = jnp.sum(grad * hat, axis=0, keepdims=True)
        sums_ref[0, 1:2] = jnp.sum(grad, axis=0, keepdims=True)
        sums_ref[0, 2:3] = jnp.sum(total, axis=0, keepdims=True)
        sums_ref[0, 3:4] = jnp.sum(cot, axis=0, keepdims=True)
        sums_ref[0, 4:8] = jnp.zeros((4, sums_ref.shape[2]), F32)


def feed(normed, cot, res, w_up, w_down, up_bias, down_bias, gain, w_out, share, padded, seq):
    group, width, local = w_up.shape
    hidden = group * local
    block = min(512, local)
    per = local // block
    tokens = share * padded
    rows = pl.BlockSpec((padded, width), lambda i, f: (i, 0))
    vector = pl.BlockSpec((1, width), lambda i, f: (0, 0))
    return pl.pallas_call(
        feed_kernel,
        grid=(share, hidden // block),
        in_specs=[
            rows,
            rows,
            rows,
            pl.BlockSpec((1, width, block), lambda i, f: (f // per, 0, f % per)),
            pl.BlockSpec((block, width), lambda i, f: (f, 0)),
            pl.BlockSpec((1, block), lambda i, f: (0, f)),
            vector,
            vector,
            pl.BlockSpec(w_out.shape, lambda i, f: (0, 0)),
        ],
        out_specs=[
            pl.BlockSpec((padded, block), lambda i, f: (i, f)),
            pl.BlockSpec((1, padded, block), lambda i, f: (f // per, i, f % per)),
            pl.BlockSpec((1, seq, width), lambda i, f: (i, 0, 0)),
            rows,
            rows,
            pl.BlockSpec((1, 8, block), lambda i, f: (i, 0, f)),
            pl.BlockSpec((1, 8, width), lambda i, f: (i, 0, 0)),
        ],
        out_shape=[
            jax.ShapeDtypeStruct((tokens, hidden), BF16),
            jax.ShapeDtypeStruct((group, tokens, local), BF16),
            jax.ShapeDtypeStruct((share, seq, width), BF16),
            jax.ShapeDtypeStruct((tokens, width), BF16),
            jax.ShapeDtypeStruct((tokens, w_out.shape[0]), BF16),
            jax.ShapeDtypeStruct((share, 8, hidden), F32),
            jax.ShapeDtypeStruct((share, 8, width), F32),
        ],
        scratch_shapes=[pltpu.VMEM((padded, width), F32), pltpu.VMEM((padded, width), F32)],
        cost_estimate=cost(8 * tokens * width * hidden * 1.4, share * 3e7),
        compiler_params=params(2),
        name="feed",
    )(normed, cot, res, w_up, w_down, up_bias, down_bias, gain, w_out)


def input_kernel(x_ref, grad_ref, w_ref, branch_ref, gain_ref, out_ref, qsum_ref, sums_ref, acc):
    step = pl.program_id(1)
    rows = x_ref.shape[1]
    grad = grad_ref[0]
    part = lax.dot_general(grad, w_ref[0], NT, preferred_element_type=F32)
    qsum_ref[0, 0] = jnp.broadcast_to(
        jnp.sum(grad.astype(F32), axis=0, keepdims=True), qsum_ref.shape[2:]
    )

    @pl.when(step == 0)
    def _():
        acc[...] = part

    @pl.when(step > 0)
    def _():
        acc[...] += part

    @pl.when(step == pl.num_programs(1) - 1)
    def _():
        hat, inverse = norm_rows(x_ref[0].astype(F32))
        normed = acc[0:rows]
        scaled = normed * gain_ref[...]
        out_ref[0] = (
            branch_ref[0:rows].astype(F32)
            + inverse
            * (
                scaled
                - jnp.mean(scaled, axis=-1, keepdims=True)
                - hat * jnp.mean(scaled * hat, axis=-1, keepdims=True)
            )
        ).astype(BF16)
        sums_ref[0, 0:1] = jnp.sum(normed * hat, axis=0, keepdims=True)
        sums_ref[0, 1:2] = jnp.sum(normed, axis=0, keepdims=True)
        sums_ref[0, 2:8] = jnp.zeros((6, sums_ref.shape[2]), F32)


def input_back(activations, grads, w_all, branch, gain, padded, first, into):
    share, seq, width = activations.shape
    planes, _, columns = w_all.shape
    operands = [activations, grads, w_all, branch, gain]
    in_specs = [
        pl.BlockSpec((1, seq, width), lambda i, j: (first, 0, 0)),
        pl.BlockSpec((1, padded, columns), lambda i, j: (j, first, 0)),
        pl.BlockSpec((1, width, columns), lambda i, j: (j, 0, 0)),
        pl.BlockSpec((padded, width), lambda i, j: (first, 0)),
        pl.BlockSpec((1, width), lambda i, j: (0, 0)),
    ]
    aliases = {}
    if into is not None:
        aliases = {len(operands): 0}
        operands.append(into)
        in_specs.append(pl.BlockSpec(memory_space=pl.ANY))

    def kernel(*refs):
        input_kernel(*refs[:5], *refs[-4:])

    return pl.pallas_call(
        kernel,
        grid=(1, planes),
        in_specs=in_specs,
        out_specs=[
            pl.BlockSpec((1, seq, width), lambda i, j: (first, 0, 0)),
            pl.BlockSpec((1, 1, 8, columns), lambda i, j: (0, j, 0, 0)),
            pl.BlockSpec((1, 8, width), lambda i, j: (0, 0, 0)),
        ],
        scratch_shapes=[pltpu.VMEM((padded, width), F32)],
        out_shape=[
            jax.ShapeDtypeStruct((share, seq, width), BF16),
            jax.ShapeDtypeStruct((1, planes, 8, columns), F32),
            jax.ShapeDtypeStruct((1, 8, width), F32),
        ],
        input_output_aliases=aliases,
        compiler_params=params(2),
        cost_estimate=cost(planes * 3.5 * padded * width * columns, planes * 3e6),
        name="input_back",
    )(*operands)


def swapped(value, axis, mask):
    size = lax.axis_size(axis)
    return lax.ppermute(value, axis, [(i, i ^ mask) for i in range(size)])


def spread_parts(value):
    size = lax.axis_size("tensor")
    return [value] + [swapped(value, "tensor", r) for r in range(1, size)]


def pair_sum(values):
    while len(values) > 1:
        values = [values[i] + values[i + 1] for i in range(0, len(values), 2)]
    return values[0]


def phases():
    size = lax.axis_size("dp")
    found, stride = [], 1
    while stride < size:
        span = min(4, size // stride)
        found.append((stride, span))
        stride *= span
    return found


def tensor_sum(parts):
    terms = [parts[0]] + [swapped(parts[r], "tensor", r) for r in range(1, len(parts))]
    return pair_sum([t.astype(F32) for t in terms]).astype(BF16)


def dp_bits():
    size = lax.axis_size("dp")
    return [1 << i for i in range(size.bit_length() - 1)]


def sum_steps(pieces):
    bits = dp_bits()
    index = lax.axis_index("dp")
    orders = [bits[i % 3 : 3] + bits[: i % 3] + bits[3:] for i in range(len(pieces))]
    held = list(pieces)
    for step in range(len(bits)):
        kept, sent = [], []
        for value, order in zip(held, orders):
            half = value.shape[0] // 2
            upper = ((index // order[step]) % 2) * half
            kept.append(lax.dynamic_slice_in_dim(value, upper, half, 0))
            sent.append(
                swapped(lax.dynamic_slice_in_dim(value, half - upper, half, 0), "dp", order[step])
            )
        sent = yield sent
        held = [(k.astype(F32) + g.astype(F32)).astype(BF16) for k, g in zip(kept, sent)]
    for step in reversed(range(len(bits))):
        sent = [swapped(value, "dp", order[step]) for value, order in zip(held, orders)]
        sent = yield sent
        joined = []
        for value, got, order in zip(held, sent, orders):
            is_upper = (index // order[step]) % 2 == 1
            joined.append(
                jnp.concatenate([jnp.where(is_upper, got, value), jnp.where(is_upper, value, got)])
            )
        held = joined
    yield held


def tie(value, flying):
    tied = lax.optimization_barrier((value,) + tuple(flying))
    return tied[0], list(tied[1:])


def after(value, *earlier):
    return lax.optimization_barrier((value,) + earlier)[0]


def per_device(
    activations,
    ln1_gain,
    ln1_bias,
    w_qkv,
    qv_bias,
    w_out,
    out_bias,
    ln2_gain,
    ln2_bias,
    w_up,
    up_bias,
    w_down,
    down_bias,
    cotangent,
):
    group = lax.axis_size("tensor")
    position = lax.axis_index("tensor")
    images, seq, width = activations.shape
    share = images // group
    padded = up_to(seq, 16)
    columns = w_qkv.shape[2]
    local = w_up.shape[1]

    def row(vector):
        return vector.astype(F32).reshape(1, -1)

    inputs = lax.dynamic_slice_in_dim(activations, position * share, share, 0)
    cot_share = lax.dynamic_slice_in_dim(cotangent, position * share, share, 0)
    wqkv_all = jnp.concatenate(spread_parts(w_qkv), axis=0)
    small_all = jnp.stack(spread_parts(jnp.concatenate([qv_bias.reshape(-1), up_bias])))
    wout_all = jnp.concatenate(spread_parts(w_out), axis=0)
    wup_all = jnp.stack(spread_parts(w_up))
    wdown_all = jnp.concatenate(spread_parts(w_down), axis=0)

    qv_all = small_all[:, : 2 * columns].reshape(group, 2, columns).astype(F32)
    up_all = small_all[:, 2 * columns :].reshape(1, group * local).astype(F32)
    add_all = jnp.stack([qv_all[:, 0], jnp.zeros_like(qv_all[:, 0]), qv_all[:, 1]], axis=1).reshape(
        group * 3, 1, columns
    )

    normed_in, qkv = project(
        inputs, row(ln1_gain), row(ln1_bias), wqkv_all, add_all, share, padded
    )
    mixed, inverse, raised = attend(qkv, share, padded, seq)
    res, normed_mid, cot = middle(
        inputs, cot_share, mixed, wout_all, row(out_bias), row(ln2_gain), row(ln2_bias),
        share, padded,
    )
    active, pre, layer_out, branch, grad_mixed, up_sums, mid_sums = feed(
        normed_mid, cot, res, wup_all, wdown_all, up_all, row(down_bias), row(ln2_gain), wout_all,
        share, padded, seq,
    )
    down = lax.dot_general(active, cot, TN, preferred_element_type=F32).astype(BF16)
    pre = after(pre, down)
    up = [
        lax.dot_general(normed_mid, pre[r], TN, preferred_element_type=F32).astype(BF16)
        for r in range(group)
    ]
    branch_w = after(branch, *up)
    out = lax.dot_general(mixed, branch_w, TN, preferred_element_type=F32).astype(BF16)
    down = tensor_sum([down[r * local : (r + 1) * local] for r in range(group)])
    up_a = tensor_sum([u[:, : local // 2] for u in up])
    up_b = tensor_sum([u[:, local // 2 :] for u in up])
    out = tensor_sum([out[r * columns : (r + 1) * columns] for r in range(group)])
    grad_mixed = after(grad_mixed, down, up_a, up_b, out)
    down, up_a = lax.psum((down, up_a), "dp")

    steps = sum_steps([out, up_b[: width // 2], up_b[width // 2 :]])
    flying = next(steps)
    pairs = group * columns // PAIR
    count = max(pairs // 2, 1)
    grads = None
    calls = [(image, pair) for image in range(share) for pair in range(0, pairs, count)]
    total = 2 * len(dp_bits())
    done = 0
    for number, (image, pair) in enumerate(calls):
        grads = attend_back(
            qkv, mixed, inverse, raised, grad_mixed, padded, image, pair, count, grads
        )
        if done < total and number + 1 < len(calls):
            grad_mixed, flying = tie(grad_mixed, flying)
            flying = steps.send(flying)
            done += 1
    in_planes = grads.reshape(qkv.shape)
    heads_w = [
        jnp.einsum("cte,td->ced", grads[r], normed_in, preferred_element_type=F32)
        .astype(BF16)
        .reshape(3 * columns, width)
        for r in range(group)
    ]
    heads_w = tensor_sum(heads_w)
    branch, heads_w, *flying = lax.optimization_barrier((branch, heads_w) + tuple(flying))
    while done < total:
        flying = steps.send(flying)
        done += 1
    out, up_b0, up_b1 = flying

    steps = sum_steps([heads_w[c * columns : (c + 1) * columns] for c in range(3)])
    flying = next(steps)
    done = 0
    grad_input, parts = None, []
    for image in range(share):
        grad_input, *sums = input_back(
            inputs, in_planes, wqkv_all, branch, row(ln1_gain), padded, image, grad_input
        )
        parts.append(sums)
        if image + 1 < share:
            branch, flying = tie(branch, flying)
            flying = steps.send(flying)
            done += 1
    while done < total:
        flying = steps.send(flying)
        done += 1
    grad_w_qkv = jnp.stack([plane.astype(F32).T for plane in flying])
    grad_w_out = out.astype(F32)
    grad_w_up = jnp.concatenate(
        [up_a.astype(F32), jnp.concatenate([up_b0, up_b1], axis=0).astype(F32)], axis=1
    )
    grad_w_down = down.astype(F32)
    qkv_sums = jnp.concatenate([p[0] for p in parts])
    in_sums = jnp.concatenate([p[1] for p in parts])
    in_sum = jnp.sum(in_sums, axis=0)
    mid_sum = jnp.sum(mid_sums, axis=0)
    qkv_sum = jnp.sum(qkv_sums[:, :, 0], axis=0).reshape(group, 3, columns)
    up_sum = jnp.sum(up_sums[:, 0], axis=0).reshape(group, local)
    shards = jnp.concatenate([qkv_sum[:, 0], qkv_sum[:, 2], up_sum], axis=1)
    shard = pair_sum([shards[0]] + [swapped(shards[r], "tensor", r) for r in range(1, group)])
    whole = jnp.concatenate([in_sum[:2], mid_sum[:4]], axis=0)
    whole = pair_sum([whole] + [swapped(whole, "tensor", r) for r in range(1, group)])
    vectors = jnp.concatenate([whole.reshape(-1), shard])
    for stride, span in phases():
        vectors = pair_sum(
            [vectors] + [swapped(vectors, "dp", r * stride) for r in range(1, span)]
        )
    whole = vectors[: 6 * width].reshape(6, width)
    rest = vectors[6 * width :]
    grad_qv = rest[: 2 * columns].reshape(2, columns)
    grad_up_bias = rest[2 * columns :]
    return (
        layer_out,
        grad_input,
        whole[0],
        whole[1],
        grad_w_qkv,
        grad_qv,
        grad_w_out,
        whole[4],
        whole[2],
        whole[3],
        grad_w_up,
        grad_up_bias,
        grad_w_down,
        whole[5],
    )


def solution(mesh):
    placed = (
        P("dp", None, None),
        P(),
        P(),
        P(None, None, "tensor"),
        P(None, "tensor"),
        P("tensor", None),
        P(),
        P(),
        P(),
        P(None, "tensor"),
        P("tensor"),
        P("tensor", None),
        P(),
        P("dp", None, None),
    )
    return jax.shard_map(
        per_device,
        mesh=mesh,
        in_specs=placed,
        out_specs=(
            P(("dp", "tensor"), None, None),
            P(("dp", "tensor"), None, None),
            P(),
            P(),
            P(None, None, "tensor"),
            P(None, "tensor"),
            P("tensor", None),
            P(),
            P(),
            P(),
            P(None, "tensor"),
            P("tensor"),
            P("tensor", None),
            P(),
        ),
        check_vma=False,
    )
```

```python
import functools

import jax
import jax.numpy as jnp
from jax import lax
from jax.experimental import pallas as pl
from jax.experimental.pallas import tpu as pltpu
from jax.sharding import PartitionSpec as P

HEAD = 64
PAIR = 2 * HEAD
EPSILON = 1e-06
ROOT_HALF = 0.7071067811865476
INV_ROOT_TWO_PI = 0.3989422804014327
MASKED = -1e30
BF16 = jnp.bfloat16
F32 = jnp.float32
VMEM_BYTES = 63 * 1024 * 1024
NT = (((1,), (1,)), ((), ()))
TN = (((0,), (0,)), ((), ()))


def up_to(count, step):
    return -(-count // step) * step


def cost(flops, moved):
    return pl.CostEstimate(flops=int(flops), bytes_accessed=int(moved), transcendentals=0)


def params(axes):
    return pltpu.CompilerParams(
        dimension_semantics=("arbitrary",) * axes, vmem_limit_bytes=VMEM_BYTES
    )


def norm_rows(rows, eps=EPSILON):
    center = rows - jnp.mean(rows, axis=-1, keepdims=True)
    inverse = lax.rsqrt(jnp.mean(center * center, axis=-1, keepdims=True) + eps)
    return center * inverse, inverse


def first_lanes():
    lane = lax.broadcasted_iota(jnp.int32, (1, PAIR), 1)
    return lane


def project_kernel(x_ref, gain_ref, bias_ref, w_ref, add_ref, normed_ref, out_ref):
    step = pl.program_id(1)
    rows = x_ref.shape[1]

    @pl.when(step == 0)
    def _():
        hat, _ = norm_rows(x_ref[0].astype(F32))
        normed_ref[...] = jnp.zeros_like(normed_ref)
        normed_ref[0:rows] = (hat * gain_ref[...] + bias_ref[...]).astype(BF16)

    normed = normed_ref[...]
    for plane in range(3):
        acc = jnp.dot(normed, w_ref[plane], preferred_element_type=F32) + add_ref[plane]
        if plane == 0:
            acc = acc * HEAD ** (-0.5)
        out_ref[plane] = acc.astype(BF16)


def project(activations, gain, bias, w_all, add_all, share, padded):
    _, seq, width = activations.shape
    planes, _, columns = w_all.shape
    return pl.pallas_call(
        project_kernel,
        grid_spec=pl.GridSpec(
            grid=(share, planes // 3),
            in_specs=[
                pl.BlockSpec((1, seq, width), lambda i, j: (i, 0, 0)),
                pl.BlockSpec((1, width), lambda i, j: (0, 0)),
                pl.BlockSpec((1, width), lambda i, j: (0, 0)),
                pl.BlockSpec((3, width, columns), lambda i, j: (j, 0, 0)),
                pl.BlockSpec((3, 1, columns), lambda i, j: (j, 0, 0)),
            ],
            out_specs=[
                pl.BlockSpec((padded, width), lambda i, j: (i, 0)),
                pl.BlockSpec((3, padded, columns), lambda i, j: (j, i, 0)),
            ],
        ),
        out_shape=[
            jax.ShapeDtypeStruct((share * padded, width), BF16),
            jax.ShapeDtypeStruct((planes, share * padded, columns), BF16),
        ],
        cost_estimate=cost(share * planes * 2 * padded * width * columns * 1.5, share * planes * 2e6),
        compiler_params=params(2),
        name="project",
    )(activations, gain, bias, w_all, add_all)


def attend_kernel(seq, keys_padded, q_ref, k_ref, v_ref, mixed_ref, inverse_ref, raised_ref):
    rows = q_ref.shape[1]
    lane = lax.broadcasted_iota(jnp.int32, (1, PAIR), 1)
    q = q_ref[0]
    extra = jnp.zeros((keys_padded - rows, PAIR), BF16)
    k = jnp.concatenate([k_ref[0], extra], axis=0)
    v = jnp.concatenate([v_ref[0], extra], axis=0)
    vx = jnp.concatenate([v, jnp.ones((keys_padded, PAIR), BF16)], axis=1)
    row = lax.broadcasted_iota(jnp.int32, (keys_padded, PAIR), 0)
    lane_k = lax.broadcasted_iota(jnp.int32, (keys_padded, PAIR), 1)
    lane_q = lax.broadcasted_iota(jnp.int32, (rows, PAIR), 1)
    results = []
    for head in range(2):
        mark = HEAD * (1 - head)
        inside_k = (lane_k // HEAD) == head
        inside_q = (lane_q // HEAD) == head
        hide = jnp.where((lane_k == mark) & (row >= seq), MASKED, 0.0).astype(BF16)
        one = jnp.where(lane_q == mark, 1.0, 0.0).astype(BF16)
        kx = jnp.where(inside_k, k, hide)
        qx = jnp.where(inside_q, q, one)
        scores = lax.dot_general(qx, kx, NT, preferred_element_type=F32)
        raised = jnp.exp(scores - jnp.max(scores, axis=-1, keepdims=True)).astype(BF16)
        raised_ref[0, head] = raised
        results.append(jnp.dot(raised, vx, preferred_element_type=F32))
    inside = (lane // HEAD) == 0
    total = jnp.where(inside, results[0][:, :PAIR], results[1][:, :PAIR])
    inverse = 1.0 / jnp.where(inside, results[0][:, PAIR:], results[1][:, PAIR:])
    mixed_ref[...] = (total * inverse).astype(BF16)
    inverse_ref[...] = inverse


def attend(qkv, share, padded, seq):
    planes, _, columns = qkv.shape
    per = columns // PAIR
    pairs = planes // 3 * per
    keys_padded = up_to(padded, 128)

    def plane(c):
        return lambda i, p: (p // per * 3 + c, i, p % per)

    return pl.pallas_call(
        functools.partial(attend_kernel, seq, keys_padded),
        grid=(share, pairs),
        in_specs=[pl.BlockSpec((1, padded, PAIR), plane(c)) for c in range(3)],
        out_specs=[
            pl.BlockSpec((padded, PAIR), lambda i, p: (i, p)),
            pl.BlockSpec((padded, PAIR), lambda i, p: (i, p)),
            pl.BlockSpec((1, 2, padded, keys_padded), lambda i, p: (i * pairs + p, 0, 0, 0)),
        ],
        out_shape=[
            jax.ShapeDtypeStruct((share * padded, pairs * PAIR), BF16),
            jax.ShapeDtypeStruct((share * padded, pairs * PAIR), F32),
            jax.ShapeDtypeStruct((share * pairs, 2, padded, keys_padded), BF16),
        ],
        cost_estimate=cost(share * pairs * 1e9, share * pairs * 3e6),
        compiler_params=params(2),
        name="attend",
    )(qkv, qkv, qkv)


def attend_back_kernel(
    keys_padded, q_ref, k_ref, v_ref, mixed_ref, inverse_ref, raised_ref, up_ref, out_ref
):
    rows = q_ref.shape[1]
    lane = lax.broadcasted_iota(jnp.int32, (1, PAIR), 1)
    lane_k = lax.broadcasted_iota(jnp.int32, (keys_padded, PAIR), 1)
    lane_q = lax.broadcasted_iota(jnp.int32, (rows, PAIR), 1)
    q = q_ref[0]
    extra = jnp.zeros((keys_padded - rows, PAIR), BF16)
    k = jnp.concatenate([k_ref[0], extra], axis=0)
    v = jnp.concatenate([v_ref[0], extra], axis=0)
    up_f = up_ref[...].astype(F32) * inverse_ref[...]
    up = up_f.astype(BF16)
    spread = pltpu.roll(-(up_f * mixed_ref[...].astype(F32)), HEAD, 1).astype(BF16)
    none = jnp.zeros_like(k)
    grad_q = None
    grad_k, grad_v = [], []
    for head in range(2):
        inside_k = (lane_k // HEAD) == head
        inside_q = (lane_q // HEAD) == head
        left = jnp.where(inside_q, up, spread)
        right = jnp.where(inside_k, v, jnp.ones_like(v))
        raised = raised_ref[0, head]
        shifted = lax.dot_general(left, right, NT, preferred_element_type=F32)
        grad_scores = (raised.astype(F32) * shifted).astype(BF16)
        part = jnp.dot(grad_scores, jnp.where(inside_k, k, none), preferred_element_type=F32)
        grad_q = part if grad_q is None else grad_q + part
        grad_k.append(lax.dot_general(grad_scores, q, TN, preferred_element_type=F32))
        grad_v.append(lax.dot_general(raised, up, TN, preferred_element_type=F32))
    inside = (lane // HEAD) == 0
    out_ref[0, 0] = (grad_q * HEAD ** (-0.5)).astype(BF16)
    out_ref[0, 1] = jnp.where(inside, grad_k[0], grad_k[1])[:rows].astype(BF16)
    out_ref[0, 2] = jnp.where(inside, grad_v[0], grad_v[1])[:rows].astype(BF16)


def attend_back(qkv, mixed, inverse, raised, upstream, share, padded):
    planes, tokens, columns = qkv.shape
    per = columns // PAIR
    pairs = planes // 3 * per
    keys_padded = up_to(padded, 128)

    def plane(c):
        return lambda i, p: (p // per * 3 + c, i, p % per)

    column = pl.BlockSpec((padded, PAIR), lambda i, p: (i, p))
    return pl.pallas_call(
        functools.partial(attend_back_kernel, keys_padded),
        grid=(share, pairs),
        in_specs=[pl.BlockSpec((1, padded, PAIR), plane(c)) for c in range(3)]
        + [
            column,
            column,
            pl.BlockSpec((1, 2, padded, keys_padded), lambda i, p: (i * pairs + p, 0, 0, 0)),
            column,
        ],
        out_specs=pl.BlockSpec((1, 3, padded, PAIR), lambda i, p: (p // per, 0, i, p % per)),
        out_shape=jax.ShapeDtypeStruct((planes // 3, 3, tokens, columns), BF16),
        compiler_params=params(2),
        cost_estimate=cost(share * pairs * 1.3e9, share * pairs * 3e6),
        name="attend_back",
    )(qkv, qkv, qkv, mixed, inverse, raised, upstream)


def middle_kernel(
    x_ref, cot_ref, mixed_ref, w_ref, add_ref, gain_ref, bias_ref, res_ref, normed_ref, cotp_ref
):
    rows = x_ref.shape[1]
    res_ref[...] = jnp.dot(mixed_ref[...], w_ref[...], preferred_element_type=F32) + add_ref[...]
    res_ref[0:rows] += x_ref[0].astype(F32)
    hat, _ = norm_rows(res_ref[...])
    normed_ref[...] = (hat * gain_ref[...] + bias_ref[...]).astype(BF16)
    cotp_ref[...] = jnp.zeros_like(cotp_ref)
    cotp_ref[0:rows] = cot_ref[0]


def middle(activations, cotangent, mixed, w_out, add, gain, bias, share, padded):
    _, seq, width = activations.shape
    vector = pl.BlockSpec((1, width), lambda i: (0, 0))
    image = pl.BlockSpec((1, seq, width), lambda i: (i, 0, 0))
    rows = pl.BlockSpec((padded, width), lambda i: (i, 0))
    tokens = share * padded
    return pl.pallas_call(
        middle_kernel,
        grid_spec=pl.GridSpec(
            grid=(share,),
            in_specs=[
                image,
                image,
                pl.BlockSpec((padded, mixed.shape[1]), lambda i: (i, 0)),
                pl.BlockSpec(w_out.shape, lambda i: (0, 0)),
                vector,
                vector,
                vector,
            ],
            out_specs=[rows, rows, rows],
        ),
        out_shape=[
            jax.ShapeDtypeStruct((tokens, width), F32),
            jax.ShapeDtypeStruct((tokens, width), BF16),
            jax.ShapeDtypeStruct((tokens, width), BF16),
        ],
        cost_estimate=cost(tokens * width * width * 6, tokens * width * 14),
        compiler_params=params(1),
        name="middle",
    )(activations, cotangent, mixed, w_out, add, gain, bias)


def feed_kernel(
    normed_ref,
    cot_ref,
    res_ref,
    wu_ref,
    wd_ref,
    ub_ref,
    db_ref,
    gain_ref,
    wo_ref,
    active_ref,
    pre_ref,
    out_ref,
    branch_ref,
    mixed_ref,
    ubsum_ref,
    sums_ref,
    feed_acc,
    normed_acc,
):
    step = pl.program_id(1)
    rows = out_ref.shape[1]
    wu = wu_ref[0]
    wd = wd_ref[...]
    hidden = jnp.dot(normed_ref[...], wu, preferred_element_type=F32) + ub_ref[...]
    back = lax.dot_general(cot_ref[...], wd, NT, preferred_element_type=F32)
    below = 0.5 * (1.0 + lax.erf(hidden * ROOT_HALF))
    slope = below + hidden * (INV_ROOT_TWO_PI * jnp.exp(-0.5 * hidden * hidden))
    active = (hidden * below).astype(BF16)
    pre_f = back * slope
    pre = pre_f.astype(BF16)
    active_ref[...] = active
    pre_ref[0] = pre
    ubsum_ref[0] = jnp.broadcast_to(jnp.sum(pre_f, axis=0, keepdims=True), ubsum_ref.shape[1:])
    feed = jnp.dot(active, wd, preferred_element_type=F32)
    normed = lax.dot_general(pre, wu, NT, preferred_element_type=F32)

    @pl.when(step == 0)
    def _():
        feed_acc[...] = feed
        normed_acc[...] = normed

    @pl.when(step > 0)
    def _():
        feed_acc[...] += feed
        normed_acc[...] += normed

    @pl.when(step == pl.num_programs(1) - 1)
    def _():
        res = res_ref[...]
        out_ref[0] = (res + feed_acc[...] + db_ref[...])[0:rows].astype(BF16)
        hat, inverse = norm_rows(res)
        grad = normed_acc[...]
        scaled = grad * gain_ref[...]
        cot = cot_ref[...].astype(F32)
        total = cot + inverse * (
            scaled
            - jnp.mean(scaled, axis=-1, keepdims=True)
            - hat * jnp.mean(scaled * hat, axis=-1, keepdims=True)
        )
        branch = total.astype(BF16)
        branch_ref[...] = branch
        mixed_ref[...] = lax.dot_general(branch, wo_ref[...], NT, preferred_element_type=F32).astype(BF16)
        sums_ref[0, 0:1] = jnp.sum(grad * hat, axis=0, keepdims=True)
        sums_ref[0, 1:2] = jnp.sum(grad, axis=0, keepdims=True)
        sums_ref[0, 2:3] = jnp.sum(total, axis=0, keepdims=True)
        sums_ref[0, 3:4] = jnp.sum(cot, axis=0, keepdims=True)
        sums_ref[0, 4:8] = jnp.zeros((4, sums_ref.shape[2]), F32)


def feed(normed, cot, res, w_up, w_down, up_bias, down_bias, gain, w_out, share, padded, seq):
    group, width, local = w_up.shape
    hidden = group * local
    block = min(512, local)
    per = local // block
    tokens = share * padded
    rows = pl.BlockSpec((padded, width), lambda i, f: (i, 0))
    vector = pl.BlockSpec((1, width), lambda i, f: (0, 0))
    return pl.pallas_call(
        feed_kernel,
        grid=(share, hidden // block),
        in_specs=[
            rows,
            rows,
            rows,
            pl.BlockSpec((1, width, block), lambda i, f: (f // per, 0, f % per)),
            pl.BlockSpec((block, width), lambda i, f: (f, 0)),
            pl.BlockSpec((1, block), lambda i, f: (0, f)),
            vector,
            vector,
            pl.BlockSpec(w_out.shape, lambda i, f: (0, 0)),
        ],
        out_specs=[
            pl.BlockSpec((padded, block), lambda i, f: (i, f)),
            pl.BlockSpec((1, padded, block), lambda i, f: (f // per, i, f % per)),
            pl.BlockSpec((1, seq, width), lambda i, f: (i, 0, 0)),
            rows,
            rows,
            pl.BlockSpec((1, 8, block), lambda i, f: (i, 0, f)),
            pl.BlockSpec((1, 8, width), lambda i, f: (i, 0, 0)),
        ],
        out_shape=[
            jax.ShapeDtypeStruct((tokens, hidden), BF16),
            jax.ShapeDtypeStruct((group, tokens, local), BF16),
            jax.ShapeDtypeStruct((share, seq, width), BF16),
            jax.ShapeDtypeStruct((tokens, width), BF16),
            jax.ShapeDtypeStruct((tokens, w_out.shape[0]), BF16),
            jax.ShapeDtypeStruct((share, 8, hidden), F32),
            jax.ShapeDtypeStruct((share, 8, width), F32),
        ],
        scratch_shapes=[pltpu.VMEM((padded, width), F32), pltpu.VMEM((padded, width), F32)],
        cost_estimate=cost(8 * tokens * width * hidden * 1.4, share * 3e7),
        compiler_params=params(2),
        name="feed",
    )(normed, cot, res, w_up, w_down, up_bias, down_bias, gain, w_out)


def input_kernel(x_ref, grad_ref, w_ref, branch_ref, gain_ref, out_ref, qsum_ref, sums_ref, acc):
    step = pl.program_id(1)
    rows = x_ref.shape[1]
    part = None
    for plane in range(3):
        grad = grad_ref[plane]
        term = lax.dot_general(grad, w_ref[plane], NT, preferred_element_type=F32)
        part = term if part is None else part + term
        if plane != 1:
            qsum_ref[0, plane] = jnp.broadcast_to(
                jnp.sum(grad.astype(F32), axis=0, keepdims=True), qsum_ref.shape[2:]
            )
        else:
            qsum_ref[0, plane] = jnp.zeros(qsum_ref.shape[2:], F32)

    @pl.when(step == 0)
    def _():
        acc[...] = part

    @pl.when(step > 0)
    def _():
        acc[...] += part

    @pl.when(step == pl.num_programs(1) - 1)
    def _():
        hat, inverse = norm_rows(x_ref[0].astype(F32))
        normed = acc[0:rows]
        scaled = normed * gain_ref[...]
        out_ref[0] = (
            branch_ref[0:rows].astype(F32)
            + inverse
            * (
                scaled
                - jnp.mean(scaled, axis=-1, keepdims=True)
                - hat * jnp.mean(scaled * hat, axis=-1, keepdims=True)
            )
        ).astype(BF16)
        sums_ref[0, 0:1] = jnp.sum(normed * hat, axis=0, keepdims=True)
        sums_ref[0, 1:2] = jnp.sum(normed, axis=0, keepdims=True)
        sums_ref[0, 2:8] = jnp.zeros((6, sums_ref.shape[2]), F32)


def input_back(activations, grads, w_all, branch, gain, padded, first, count, into):
    share, seq, width = activations.shape
    planes, _, columns = w_all.shape
    operands = [activations, grads, w_all, branch, gain]
    in_specs = [
        pl.BlockSpec((1, seq, width), lambda i, j: (first + i, 0, 0)),
        pl.BlockSpec((3, padded, columns), lambda i, j: (j, first + i, 0)),
        pl.BlockSpec((3, width, columns), lambda i, j: (j, 0, 0)),
        pl.BlockSpec((padded, width), lambda i, j: (first + i, 0)),
        pl.BlockSpec((1, width), lambda i, j: (0, 0)),
    ]
    aliases = {}
    if into is not None:
        aliases = {len(operands): 0}
        operands.append(into)
        in_specs.append(pl.BlockSpec(memory_space=pl.ANY))

    def kernel(*refs):
        input_kernel(*refs[:5], *refs[-4:])

    return pl.pallas_call(
        kernel,
        grid=(count, planes // 3),
        in_specs=in_specs,
        out_specs=[
            pl.BlockSpec((1, seq, width), lambda i, j: (first + i, 0, 0)),
            pl.BlockSpec((1, 3, 8, columns), lambda i, j: (i, j, 0, 0)),
            pl.BlockSpec((1, 8, width), lambda i, j: (i, 0, 0)),
        ],
        scratch_shapes=[pltpu.VMEM((padded, width), F32)],
        out_shape=[
            jax.ShapeDtypeStruct((share, seq, width), BF16),
            jax.ShapeDtypeStruct((count, planes, 8, columns), F32),
            jax.ShapeDtypeStruct((count, 8, width), F32),
        ],
        input_output_aliases=aliases,
        compiler_params=params(2),
        cost_estimate=cost(count * planes * 3.5 * padded * width * columns, count * planes * 3e6),
        name="input_back",
    )(*operands)


def swapped(value, axis, mask):
    size = lax.axis_size(axis)
    return lax.ppermute(value, axis, [(i, i ^ mask) for i in range(size)])


def spread_parts(value):
    size = lax.axis_size("tensor")
    return [value] + [swapped(value, "tensor", r) for r in range(1, size)]


def pair_sum(values):
    while len(values) > 1:
        values = [values[i] + values[i + 1] for i in range(0, len(values), 2)]
    return values[0]


def phases():
    size = lax.axis_size("dp")
    found, stride = [], 1
    while stride < size:
        span = min(4, size // stride)
        found.append((stride, span))
        stride *= span
    return found


def tensor_sum(parts):
    terms = [parts[0]] + [swapped(parts[r], "tensor", r) for r in range(1, len(parts))]
    return pair_sum([t.astype(F32) for t in terms]).astype(BF16)


def dp_bits():
    size = lax.axis_size("dp")
    return [1 << i for i in range(size.bit_length() - 1)]


def sum_steps(pieces):
    bits = dp_bits()
    index = lax.axis_index("dp")
    orders = [bits[i % 3 : 3] + bits[: i % 3] + bits[3:] for i in range(len(pieces))]
    held = list(pieces)
    for step in range(len(bits)):
        kept, sent = [], []
        for value, order in zip(held, orders):
            half = value.shape[0] // 2
            upper = ((index // order[step]) % 2) * half
            kept.append(lax.dynamic_slice_in_dim(value, upper, half, 0))
            sent.append(
                swapped(lax.dynamic_slice_in_dim(value, half - upper, half, 0), "dp", order[step])
            )
        sent = yield sent
        held = [(k.astype(F32) + g.astype(F32)).astype(BF16) for k, g in zip(kept, sent)]
    for step in reversed(range(len(bits))):
        sent = [swapped(value, "dp", order[step]) for value, order in zip(held, orders)]
        sent = yield sent
        joined = []
        for value, got, order in zip(held, sent, orders):
            is_upper = (index // order[step]) % 2 == 1
            joined.append(
                jnp.concatenate([jnp.where(is_upper, got, value), jnp.where(is_upper, value, got)])
            )
        held = joined
    yield held


def tie(value, flying):
    tied = lax.optimization_barrier((value,) + tuple(flying))
    return tied[0], list(tied[1:])


def after(value, *earlier):
    return lax.optimization_barrier((value,) + earlier)[0]


def per_device(
    activations,
    ln1_gain,
    ln1_bias,
    w_qkv,
    qv_bias,
    w_out,
    out_bias,
    ln2_gain,
    ln2_bias,
    w_up,
    up_bias,
    w_down,
    down_bias,
    cotangent,
):
    group = lax.axis_size("tensor")
    position = lax.axis_index("tensor")
    images, seq, width = activations.shape
    share = images // group
    padded = up_to(seq, 16)
    columns = w_qkv.shape[2]
    local = w_up.shape[1]

    def row(vector):
        return vector.astype(F32).reshape(1, -1)

    inputs = lax.dynamic_slice_in_dim(activations, position * share, share, 0)
    cot_share = lax.dynamic_slice_in_dim(cotangent, position * share, share, 0)
    wqkv_all = jnp.concatenate(spread_parts(w_qkv), axis=0)
    small_all = jnp.stack(spread_parts(jnp.concatenate([qv_bias.reshape(-1), up_bias])))
    wout_all = jnp.concatenate(spread_parts(w_out), axis=0)
    wup_all = jnp.stack(spread_parts(w_up))
    wdown_all = jnp.concatenate(spread_parts(w_down), axis=0)

    qv_all = small_all[:, : 2 * columns].reshape(group, 2, columns).astype(F32)
    up_all = small_all[:, 2 * columns :].reshape(1, group * local).astype(F32)
    add_all = jnp.stack([qv_all[:, 0], jnp.zeros_like(qv_all[:, 0]), qv_all[:, 1]], axis=1).reshape(
        group * 3, 1, columns
    )

    normed_in, qkv = project(
        inputs, row(ln1_gain), row(ln1_bias), wqkv_all, add_all, share, padded
    )
    mixed, inverse, raised = attend(qkv, share, padded, seq)
    res, normed_mid, cot = middle(
        inputs, cot_share, mixed, wout_all, row(out_bias), row(ln2_gain), row(ln2_bias),
        share, padded,
    )
    active, pre, layer_out, branch, grad_mixed, up_sums, mid_sums = feed(
        normed_mid, cot, res, wup_all, wdown_all, up_all, row(down_bias), row(ln2_gain), wout_all,
        share, padded, seq,
    )
    down = lax.dot_general(active, cot, TN, preferred_element_type=F32).astype(BF16)
    pre = after(pre, down)
    up = [
        lax.dot_general(normed_mid, pre[r], TN, preferred_element_type=F32).astype(BF16)
        for r in range(group)
    ]
    down = tensor_sum([down[r * local : (r + 1) * local] for r in range(group)])
    branch_w = after(branch, down, *up)
    out = lax.dot_general(mixed, branch_w, TN, preferred_element_type=F32).astype(BF16)
    up = tensor_sum(up)
    grad_mixed = after(grad_mixed, down, up, out)
    down, up = lax.psum((down, up), "dp")
    out = tensor_sum([out[r * columns : (r + 1) * columns] for r in range(group)])
    grads = attend_back(qkv, mixed, inverse, raised, grad_mixed, share, padded)
    in_planes = grads.reshape(qkv.shape)
    heads_w = [
        jnp.einsum("cte,td->ced", grads[r], normed_in, preferred_element_type=F32)
        .astype(BF16)
        .reshape(3 * columns, width)
        for r in range(group)
    ]
    heads_w = tensor_sum(heads_w)
    branch, heads_w, out = lax.optimization_barrier((branch, heads_w, out))

    steps = sum_steps([heads_w[c * columns : (c + 1) * columns] for c in range(3)] + [out])
    flying = next(steps)
    total = 2 * len(dp_bits())
    done = 0
    grad_input, parts = None, []
    half = max(share // 2, 1)
    for image in range(0, share, half):
        grad_input, *sums = input_back(
            inputs, in_planes, wqkv_all, branch, row(ln1_gain), padded, image, half, grad_input
        )
        parts.append(sums)
        if image + half < share:
            branch, flying = tie(branch, flying)
            flying = steps.send(flying)
            done += 1
    while done < total:
        flying = steps.send(flying)
        done += 1
    grad_w_qkv = jnp.stack([plane.astype(F32).T for plane in flying[:3]])
    grad_w_out = flying[3].astype(F32)
    grad_w_up = up.astype(F32)
    grad_w_down = down.astype(F32)
    qkv_sums = jnp.concatenate([p[0] for p in parts])
    in_sums = jnp.concatenate([p[1] for p in parts])
    in_sum = jnp.sum(in_sums, axis=0)
    mid_sum = jnp.sum(mid_sums, axis=0)
    qkv_sum = jnp.sum(qkv_sums[:, :, 0], axis=0).reshape(group, 3, columns)
    up_sum = jnp.sum(up_sums[:, 0], axis=0).reshape(group, local)
    shards = jnp.concatenate([qkv_sum[:, 0], qkv_sum[:, 2], up_sum], axis=1)
    shard = pair_sum([shards[0]] + [swapped(shards[r], "tensor", r) for r in range(1, group)])
    whole = jnp.concatenate([in_sum[:2], mid_sum[:4]], axis=0)
    whole = pair_sum([whole] + [swapped(whole, "tensor", r) for r in range(1, group)])
    vectors = jnp.concatenate([whole.reshape(-1), shard])
    for stride, span in phases():
        vectors = pair_sum(
            [vectors] + [swapped(vectors, "dp", r * stride) for r in range(1, span)]
        )
    whole = vectors[: 6 * width].reshape(6, width)
    rest = vectors[6 * width :]
    grad_qv = rest[: 2 * columns].reshape(2, columns)
    grad_up_bias = rest[2 * columns :]
    return (
        layer_out,
        grad_input,
        whole[0],
        whole[1],
        grad_w_qkv,
        grad_qv,
        grad_w_out,
        whole[4],
        whole[2],
        whole[3],
        grad_w_up,
        grad_up_bias,
        grad_w_down,
        whole[5],
    )


def solution(mesh):
    placed = (
        P("dp", None, None),
        P(),
        P(),
        P(None, None, "tensor"),
        P(None, "tensor"),
        P("tensor", None),
        P(),
        P(),
        P(),
        P(None, "tensor"),
        P("tensor"),
        P("tensor", None),
        P(),
        P("dp", None, None),
    )
    return jax.shard_map(
        per_device,
        mesh=mesh,
        in_specs=placed,
        out_specs=(
            P(("dp", "tensor"), None, None),
            P(("dp", "tensor"), None, None),
            P(),
            P(),
            P(None, None, "tensor"),
            P(None, "tensor"),
            P("tensor", None),
            P(),
            P(),
            P(),
            P(None, "tensor"),
            P("tensor"),
            P("tensor", None),
            P(),
        ),
        check_vma=False,
    )
```

```python
import functools

import jax
import jax.numpy as jnp
from jax import lax
from jax.experimental import pallas as pl
from jax.experimental.pallas import tpu as pltpu
from jax.sharding import PartitionSpec as P

HEAD = 64
PAIR = 2 * HEAD
EPSILON = 1e-06
ROOT_HALF = 0.7071067811865476
INV_ROOT_TWO_PI = 0.3989422804014327
MASKED = -1e30
BF16 = jnp.bfloat16
F32 = jnp.float32
VMEM_BYTES = 63 * 1024 * 1024
NT = (((1,), (1,)), ((), ()))
TN = (((0,), (0,)), ((), ()))


def up_to(count, step):
    return -(-count // step) * step


def cost(flops, moved):
    return pl.CostEstimate(flops=int(flops), bytes_accessed=int(moved), transcendentals=0)


def params(axes):
    return pltpu.CompilerParams(
        dimension_semantics=("arbitrary",) * axes, vmem_limit_bytes=VMEM_BYTES
    )


def norm_rows(rows, eps=EPSILON):
    center = rows - jnp.mean(rows, axis=-1, keepdims=True)
    inverse = lax.rsqrt(jnp.mean(center * center, axis=-1, keepdims=True) + eps)
    return center * inverse, inverse


def first_lanes():
    lane = lax.broadcasted_iota(jnp.int32, (1, PAIR), 1)
    return lane


def project_kernel(x_ref, gain_ref, bias_ref, w_ref, add_ref, normed_ref, out_ref):
    step = pl.program_id(1)
    rows = x_ref.shape[1]

    @pl.when(step == 0)
    def _():
        hat, _ = norm_rows(x_ref[0].astype(F32))
        normed_ref[...] = jnp.zeros_like(normed_ref)
        normed_ref[0:rows] = (hat * gain_ref[...] + bias_ref[...]).astype(BF16)

    normed = normed_ref[...]
    for plane in range(3):
        acc = jnp.dot(normed, w_ref[plane], preferred_element_type=F32) + add_ref[plane]
        if plane == 0:
            acc = acc * HEAD ** (-0.5)
        out_ref[plane] = acc.astype(BF16)


def project(activations, gain, bias, w_all, add_all, share, padded):
    _, seq, width = activations.shape
    planes, _, columns = w_all.shape
    return pl.pallas_call(
        project_kernel,
        grid_spec=pl.GridSpec(
            grid=(share, planes // 3),
            in_specs=[
                pl.BlockSpec((1, seq, width), lambda i, j: (i, 0, 0)),
                pl.BlockSpec((1, width), lambda i, j: (0, 0)),
                pl.BlockSpec((1, width), lambda i, j: (0, 0)),
                pl.BlockSpec((3, width, columns), lambda i, j: (j, 0, 0)),
                pl.BlockSpec((3, 1, columns), lambda i, j: (j, 0, 0)),
            ],
            out_specs=[
                pl.BlockSpec((padded, width), lambda i, j: (i, 0)),
                pl.BlockSpec((3, padded, columns), lambda i, j: (j, i, 0)),
            ],
        ),
        out_shape=[
            jax.ShapeDtypeStruct((share * padded, width), BF16),
            jax.ShapeDtypeStruct((planes, share * padded, columns), BF16),
        ],
        cost_estimate=cost(share * planes * 2 * padded * width * columns * 1.5, share * planes * 2e6),
        compiler_params=params(2),
        name="project",
    )(activations, gain, bias, w_all, add_all)


def attend_kernel(seq, keys_padded, q_ref, k_ref, v_ref, mixed_ref, inverse_ref, raised_ref):
    rows = q_ref.shape[1]
    lane = lax.broadcasted_iota(jnp.int32, (1, PAIR), 1)
    q = q_ref[0]
    extra = jnp.zeros((keys_padded - rows, PAIR), BF16)
    k = jnp.concatenate([k_ref[0], extra], axis=0)
    v = jnp.concatenate([v_ref[0], extra], axis=0)
    vx = jnp.concatenate([v, jnp.ones((keys_padded, PAIR), BF16)], axis=1)
    row = lax.broadcasted_iota(jnp.int32, (keys_padded, PAIR), 0)
    lane_k = lax.broadcasted_iota(jnp.int32, (keys_padded, PAIR), 1)
    lane_q = lax.broadcasted_iota(jnp.int32, (rows, PAIR), 1)
    results = []
    for head in range(2):
        mark = HEAD * (1 - head)
        inside_k = (lane_k // HEAD) == head
        inside_q = (lane_q // HEAD) == head
        hide = jnp.where((lane_k == mark) & (row >= seq), MASKED, 0.0).astype(BF16)
        one = jnp.where(lane_q == mark, 1.0, 0.0).astype(BF16)
        kx = jnp.where(inside_k, k, hide)
        qx = jnp.where(inside_q, q, one)
        scores = lax.dot_general(qx, kx, NT, preferred_element_type=F32)
        raised = jnp.exp(scores - jnp.max(scores, axis=-1, keepdims=True)).astype(BF16)
        raised_ref[0, head] = raised
        results.append(jnp.dot(raised, vx, preferred_element_type=F32))
    inside = (lane // HEAD) == 0
    total = jnp.where(inside, results[0][:, :PAIR], results[1][:, :PAIR])
    inverse = 1.0 / jnp.where(inside, results[0][:, PAIR:], results[1][:, PAIR:])
    mixed_ref[...] = (total * inverse).astype(BF16)
    inverse_ref[...] = inverse


def attend(qkv, share, padded, seq):
    planes, _, columns = qkv.shape
    per = columns // PAIR
    pairs = planes // 3 * per
    keys_padded = up_to(padded, 128)

    def plane(c):
        return lambda i, p: (p // per * 3 + c, i, p % per)

    return pl.pallas_call(
        functools.partial(attend_kernel, seq, keys_padded),
        grid=(share, pairs),
        in_specs=[pl.BlockSpec((1, padded, PAIR), plane(c)) for c in range(3)],
        out_specs=[
            pl.BlockSpec((padded, PAIR), lambda i, p: (i, p)),
            pl.BlockSpec((padded, PAIR), lambda i, p: (i, p)),
            pl.BlockSpec((1, 2, padded, keys_padded), lambda i, p: (i * pairs + p, 0, 0, 0)),
        ],
        out_shape=[
            jax.ShapeDtypeStruct((share * padded, pairs * PAIR), BF16),
            jax.ShapeDtypeStruct((share * padded, pairs * PAIR), F32),
            jax.ShapeDtypeStruct((share * pairs, 2, padded, keys_padded), BF16),
        ],
        cost_estimate=cost(share * pairs * 1e9, share * pairs * 3e6),
        compiler_params=params(2),
        name="attend",
    )(qkv, qkv, qkv)


def attend_back_kernel(
    keys_padded, q_ref, k_ref, v_ref, mixed_ref, inverse_ref, raised_ref, up_ref, out_ref
):
    rows = q_ref.shape[1]
    lane = lax.broadcasted_iota(jnp.int32, (1, PAIR), 1)
    lane_k = lax.broadcasted_iota(jnp.int32, (keys_padded, PAIR), 1)
    lane_q = lax.broadcasted_iota(jnp.int32, (rows, PAIR), 1)
    q = q_ref[0]
    extra = jnp.zeros((keys_padded - rows, PAIR), BF16)
    k = jnp.concatenate([k_ref[0], extra], axis=0)
    v = jnp.concatenate([v_ref[0], extra], axis=0)
    up_f = up_ref[...].astype(F32) * inverse_ref[...]
    up = up_f.astype(BF16)
    spread = pltpu.roll(-(up_f * mixed_ref[...].astype(F32)), HEAD, 1).astype(BF16)
    none = jnp.zeros_like(k)
    grad_q = None
    grad_k, grad_v = [], []
    for head in range(2):
        inside_k = (lane_k // HEAD) == head
        inside_q = (lane_q // HEAD) == head
        left = jnp.where(inside_q, up, spread)
        right = jnp.where(inside_k, v, jnp.ones_like(v))
        raised = raised_ref[0, head]
        shifted = lax.dot_general(left, right, NT, preferred_element_type=F32)
        grad_scores = (raised.astype(F32) * shifted).astype(BF16)
        part = jnp.dot(grad_scores, jnp.where(inside_k, k, none), preferred_element_type=F32)
        grad_q = part if grad_q is None else grad_q + part
        grad_k.append(lax.dot_general(grad_scores, q, TN, preferred_element_type=F32))
        grad_v.append(lax.dot_general(raised, up, TN, preferred_element_type=F32))
    inside = (lane // HEAD) == 0
    out_ref[0, 0] = (grad_q * HEAD ** (-0.5)).astype(BF16)
    out_ref[0, 1] = jnp.where(inside, grad_k[0], grad_k[1])[:rows].astype(BF16)
    out_ref[0, 2] = jnp.where(inside, grad_v[0], grad_v[1])[:rows].astype(BF16)


def attend_back(qkv, mixed, inverse, raised, upstream, share, padded):
    planes, tokens, columns = qkv.shape
    per = columns // PAIR
    pairs = planes // 3 * per
    keys_padded = up_to(padded, 128)

    def plane(c):
        return lambda i, p: (p // per * 3 + c, i, p % per)

    column = pl.BlockSpec((padded, PAIR), lambda i, p: (i, p))
    return pl.pallas_call(
        functools.partial(attend_back_kernel, keys_padded),
        grid=(share, pairs),
        in_specs=[pl.BlockSpec((1, padded, PAIR), plane(c)) for c in range(3)]
        + [
            column,
            column,
            pl.BlockSpec((1, 2, padded, keys_padded), lambda i, p: (i * pairs + p, 0, 0, 0)),
            column,
        ],
        out_specs=pl.BlockSpec((1, 3, padded, PAIR), lambda i, p: (p // per, 0, i, p % per)),
        out_shape=jax.ShapeDtypeStruct((planes // 3, 3, tokens, columns), BF16),
        compiler_params=params(2),
        cost_estimate=cost(share * pairs * 1.3e9, share * pairs * 3e6),
        name="attend_back",
    )(qkv, qkv, qkv, mixed, inverse, raised, upstream)


def middle_kernel(
    x_ref, cot_ref, mixed_ref, w_ref, add_ref, gain_ref, bias_ref, res_ref, normed_ref, cotp_ref
):
    rows = x_ref.shape[1]
    res_ref[...] = jnp.dot(mixed_ref[...], w_ref[...], preferred_element_type=F32) + add_ref[...]
    res_ref[0:rows] += x_ref[0].astype(F32)
    hat, _ = norm_rows(res_ref[...])
    normed_ref[...] = (hat * gain_ref[...] + bias_ref[...]).astype(BF16)
    cotp_ref[...] = jnp.zeros_like(cotp_ref)
    cotp_ref[0:rows] = cot_ref[0]


def middle(activations, cotangent, mixed, w_out, add, gain, bias, share, padded):
    _, seq, width = activations.shape
    vector = pl.BlockSpec((1, width), lambda i: (0, 0))
    image = pl.BlockSpec((1, seq, width), lambda i: (i, 0, 0))
    rows = pl.BlockSpec((padded, width), lambda i: (i, 0))
    tokens = share * padded
    return pl.pallas_call(
        middle_kernel,
        grid_spec=pl.GridSpec(
            grid=(share,),
            in_specs=[
                image,
                image,
                pl.BlockSpec((padded, mixed.shape[1]), lambda i: (i, 0)),
                pl.BlockSpec(w_out.shape, lambda i: (0, 0)),
                vector,
                vector,
                vector,
            ],
            out_specs=[rows, rows, rows],
        ),
        out_shape=[
            jax.ShapeDtypeStruct((tokens, width), F32),
            jax.ShapeDtypeStruct((tokens, width), BF16),
            jax.ShapeDtypeStruct((tokens, width), BF16),
        ],
        cost_estimate=cost(tokens * width * width * 6, tokens * width * 14),
        compiler_params=params(1),
        name="middle",
    )(activations, cotangent, mixed, w_out, add, gain, bias)


def feed_kernel(
    normed_ref,
    cot_ref,
    res_ref,
    wu_ref,
    wd_ref,
    ub_ref,
    db_ref,
    gain_ref,
    wo_ref,
    active_ref,
    pre_ref,
    out_ref,
    branch_ref,
    mixed_ref,
    ubsum_ref,
    sums_ref,
    feed_acc,
    normed_acc,
):
    step = pl.program_id(1)
    rows = out_ref.shape[1]
    wu = wu_ref[0]
    wd = wd_ref[...]
    hidden = jnp.dot(normed_ref[...], wu, preferred_element_type=F32) + ub_ref[...]
    back = lax.dot_general(cot_ref[...], wd, NT, preferred_element_type=F32)
    below = 0.5 * (1.0 + lax.erf(hidden * ROOT_HALF))
    slope = below + hidden * (INV_ROOT_TWO_PI * jnp.exp(-0.5 * hidden * hidden))
    active = (hidden * below).astype(BF16)
    pre_f = back * slope
    pre = pre_f.astype(BF16)
    active_ref[...] = active
    pre_ref[0] = pre
    ubsum_ref[0] = jnp.broadcast_to(jnp.sum(pre_f, axis=0, keepdims=True), ubsum_ref.shape[1:])
    feed = jnp.dot(active, wd, preferred_element_type=F32)
    normed = lax.dot_general(pre, wu, NT, preferred_element_type=F32)

    @pl.when(step == 0)
    def _():
        feed_acc[...] = feed
        normed_acc[...] = normed

    @pl.when(step > 0)
    def _():
        feed_acc[...] += feed
        normed_acc[...] += normed

    @pl.when(step == pl.num_programs(1) - 1)
    def _():
        res = res_ref[...]
        out_ref[0] = (res + feed_acc[...] + db_ref[...])[0:rows].astype(BF16)
        hat, inverse = norm_rows(res)
        grad = normed_acc[...]
        scaled = grad * gain_ref[...]
        cot = cot_ref[...].astype(F32)
        total = cot + inverse * (
            scaled
            - jnp.mean(scaled, axis=-1, keepdims=True)
            - hat * jnp.mean(scaled * hat, axis=-1, keepdims=True)
        )
        branch = total.astype(BF16)
        branch_ref[...] = branch
        mixed_ref[...] = lax.dot_general(branch, wo_ref[...], NT, preferred_element_type=F32).astype(BF16)
        sums_ref[0, 0:1] = jnp.sum(grad * hat, axis=0, keepdims=True)
        sums_ref[0, 1:2] = jnp.sum(grad, axis=0, keepdims=True)
        sums_ref[0, 2:3] = jnp.sum(total, axis=0, keepdims=True)
        sums_ref[0, 3:4] = jnp.sum(cot, axis=0, keepdims=True)
        sums_ref[0, 4:8] = jnp.zeros((4, sums_ref.shape[2]), F32)


def feed(normed, cot, res, w_up, w_down, up_bias, down_bias, gain, w_out, share, padded, seq):
    group, width, local = w_up.shape
    hidden = group * local
    block = min(512, local)
    per = local // block
    tokens = share * padded
    rows = pl.BlockSpec((padded, width), lambda i, f: (i, 0))
    vector = pl.BlockSpec((1, width), lambda i, f: (0, 0))
    return pl.pallas_call(
        feed_kernel,
        grid=(share, hidden // block),
        in_specs=[
            rows,
            rows,
            rows,
            pl.BlockSpec((1, width, block), lambda i, f: (f // per, 0, f % per)),
            pl.BlockSpec((block, width), lambda i, f: (f, 0)),
            pl.BlockSpec((1, block), lambda i, f: (0, f)),
            vector,
            vector,
            pl.BlockSpec(w_out.shape, lambda i, f: (0, 0)),
        ],
        out_specs=[
            pl.BlockSpec((padded, block), lambda i, f: (i, f)),
            pl.BlockSpec((1, padded, block), lambda i, f: (f // per, i, f % per)),
            pl.BlockSpec((1, seq, width), lambda i, f: (i, 0, 0)),
            rows,
            rows,
            pl.BlockSpec((1, 8, block), lambda i, f: (i, 0, f)),
            pl.BlockSpec((1, 8, width), lambda i, f: (i, 0, 0)),
        ],
        out_shape=[
            jax.ShapeDtypeStruct((tokens, hidden), BF16),
            jax.ShapeDtypeStruct((group, tokens, local), BF16),
            jax.ShapeDtypeStruct((share, seq, width), BF16),
            jax.ShapeDtypeStruct((tokens, width), BF16),
            jax.ShapeDtypeStruct((tokens, w_out.shape[0]), BF16),
            jax.ShapeDtypeStruct((share, 8, hidden), F32),
            jax.ShapeDtypeStruct((share, 8, width), F32),
        ],
        scratch_shapes=[pltpu.VMEM((padded, width), F32), pltpu.VMEM((padded, width), F32)],
        cost_estimate=cost(8 * tokens * width * hidden * 1.4, share * 3e7),
        compiler_params=params(2),
        name="feed",
    )(normed, cot, res, w_up, w_down, up_bias, down_bias, gain, w_out)


def input_kernel(x_ref, grad_ref, w_ref, branch_ref, gain_ref, out_ref, qsum_ref, sums_ref, acc):
    step = pl.program_id(1)
    rows = x_ref.shape[1]
    part = None
    for plane in range(3):
        grad = grad_ref[plane]
        term = lax.dot_general(grad, w_ref[plane], NT, preferred_element_type=F32)
        part = term if part is None else part + term
        if plane != 1:
            qsum_ref[0, plane] = jnp.broadcast_to(
                jnp.sum(grad.astype(F32), axis=0, keepdims=True), qsum_ref.shape[2:]
            )
        else:
            qsum_ref[0, plane] = jnp.zeros(qsum_ref.shape[2:], F32)

    @pl.when(step == 0)
    def _():
        acc[...] = part

    @pl.when(step > 0)
    def _():
        acc[...] += part

    @pl.when(step == pl.num_programs(1) - 1)
    def _():
        hat, inverse = norm_rows(x_ref[0].astype(F32))
        normed = acc[0:rows]
        scaled = normed * gain_ref[...]
        out_ref[0] = (
            branch_ref[0:rows].astype(F32)
            + inverse
            * (
                scaled
                - jnp.mean(scaled, axis=-1, keepdims=True)
                - hat * jnp.mean(scaled * hat, axis=-1, keepdims=True)
            )
        ).astype(BF16)
        sums_ref[0, 0:1] = jnp.sum(normed * hat, axis=0, keepdims=True)
        sums_ref[0, 1:2] = jnp.sum(normed, axis=0, keepdims=True)
        sums_ref[0, 2:8] = jnp.zeros((6, sums_ref.shape[2]), F32)


def input_back(activations, grads, w_all, branch, gain, padded, first, count, into):
    share, seq, width = activations.shape
    planes, _, columns = w_all.shape
    operands = [activations, grads, w_all, branch, gain]
    in_specs = [
        pl.BlockSpec((1, seq, width), lambda i, j: (first + i, 0, 0)),
        pl.BlockSpec((3, padded, columns), lambda i, j: (j, first + i, 0)),
        pl.BlockSpec((3, width, columns), lambda i, j: (j, 0, 0)),
        pl.BlockSpec((padded, width), lambda i, j: (first + i, 0)),
        pl.BlockSpec((1, width), lambda i, j: (0, 0)),
    ]
    aliases = {}
    if into is not None:
        aliases = {len(operands): 0}
        operands.append(into)
        in_specs.append(pl.BlockSpec(memory_space=pl.ANY))

    def kernel(*refs):
        input_kernel(*refs[:5], *refs[-4:])

    return pl.pallas_call(
        kernel,
        grid=(count, planes // 3),
        in_specs=in_specs,
        out_specs=[
            pl.BlockSpec((1, seq, width), lambda i, j: (first + i, 0, 0)),
            pl.BlockSpec((1, 3, 8, columns), lambda i, j: (i, j, 0, 0)),
            pl.BlockSpec((1, 8, width), lambda i, j: (i, 0, 0)),
        ],
        scratch_shapes=[pltpu.VMEM((padded, width), F32)],
        out_shape=[
            jax.ShapeDtypeStruct((share, seq, width), BF16),
            jax.ShapeDtypeStruct((count, planes, 8, columns), F32),
            jax.ShapeDtypeStruct((count, 8, width), F32),
        ],
        input_output_aliases=aliases,
        compiler_params=params(2),
        cost_estimate=cost(count * planes * 3.5 * padded * width * columns, count * planes * 3e6),
        name="input_back",
    )(*operands)


def swapped(value, axis, mask):
    size = lax.axis_size(axis)
    return lax.ppermute(value, axis, [(i, i ^ mask) for i in range(size)])


def spread_parts(value):
    size = lax.axis_size("tensor")
    return [value] + [swapped(value, "tensor", r) for r in range(1, size)]


def pair_sum(values):
    while len(values) > 1:
        values = [values[i] + values[i + 1] for i in range(0, len(values), 2)]
    return values[0]


def phases():
    size = lax.axis_size("dp")
    found, stride = [], 1
    while stride < size:
        span = min(4, size // stride)
        found.append((stride, span))
        stride *= span
    return found


def tensor_sum(parts):
    terms = [parts[0]] + [swapped(parts[r], "tensor", r) for r in range(1, len(parts))]
    return pair_sum([t.astype(F32) for t in terms]).astype(BF16)


def dp_bits():
    size = lax.axis_size("dp")
    return [1 << i for i in range(size.bit_length() - 1)]


def sum_steps(pieces):
    bits = dp_bits()
    index = lax.axis_index("dp")
    orders = [bits[i % 3 : 3] + bits[: i % 3] + bits[3:] for i in range(len(pieces))]
    held = list(pieces)
    for step in range(len(bits)):
        kept, sent = [], []
        for value, order in zip(held, orders):
            half = value.shape[0] // 2
            upper = ((index // order[step]) % 2) * half
            kept.append(lax.dynamic_slice_in_dim(value, upper, half, 0))
            sent.append(
                swapped(lax.dynamic_slice_in_dim(value, half - upper, half, 0), "dp", order[step])
            )
        sent = yield sent
        held = [(k.astype(F32) + g.astype(F32)).astype(BF16) for k, g in zip(kept, sent)]
    for step in reversed(range(len(bits))):
        sent = [swapped(value, "dp", order[step]) for value, order in zip(held, orders)]
        sent = yield sent
        joined = []
        for value, got, order in zip(held, sent, orders):
            is_upper = (index // order[step]) % 2 == 1
            joined.append(
                jnp.concatenate([jnp.where(is_upper, got, value), jnp.where(is_upper, value, got)])
            )
        held = joined
    yield held


def tie(value, flying):
    tied = lax.optimization_barrier((value,) + tuple(flying))
    return tied[0], list(tied[1:])


def after(value, *earlier):
    return lax.optimization_barrier((value,) + earlier)[0]


def per_device(
    activations,
    ln1_gain,
    ln1_bias,
    w_qkv,
    qv_bias,
    w_out,
    out_bias,
    ln2_gain,
    ln2_bias,
    w_up,
    up_bias,
    w_down,
    down_bias,
    cotangent,
):
    group = lax.axis_size("tensor")
    position = lax.axis_index("tensor")
    images, seq, width = activations.shape
    share = images // group
    padded = up_to(seq, 16)
    columns = w_qkv.shape[2]
    local = w_up.shape[1]

    def row(vector):
        return vector.astype(F32).reshape(1, -1)

    inputs = lax.dynamic_slice_in_dim(activations, position * share, share, 0)
    cot_share = lax.dynamic_slice_in_dim(cotangent, position * share, share, 0)
    wqkv_all = jnp.concatenate(spread_parts(w_qkv), axis=0)
    small_all = jnp.stack(spread_parts(jnp.concatenate([qv_bias.reshape(-1), up_bias])))
    wout_all = jnp.concatenate(spread_parts(w_out), axis=0)
    wup_all = jnp.stack(spread_parts(w_up))
    wdown_all = jnp.concatenate(spread_parts(w_down), axis=0)

    qv_all = small_all[:, : 2 * columns].reshape(group, 2, columns).astype(F32)
    up_all = small_all[:, 2 * columns :].reshape(1, group * local).astype(F32)
    add_all = jnp.stack([qv_all[:, 0], jnp.zeros_like(qv_all[:, 0]), qv_all[:, 1]], axis=1).reshape(
        group * 3, 1, columns
    )

    normed_in, qkv = project(
        inputs, row(ln1_gain), row(ln1_bias), wqkv_all, add_all, share, padded
    )
    mixed, inverse, raised = attend(qkv, share, padded, seq)
    res, normed_mid, cot = middle(
        inputs, cot_share, mixed, wout_all, row(out_bias), row(ln2_gain), row(ln2_bias),
        share, padded,
    )
    active, pre, layer_out, branch, grad_mixed, up_sums, mid_sums = feed(
        normed_mid, cot, res, wup_all, wdown_all, up_all, row(down_bias), row(ln2_gain), wout_all,
        share, padded, seq,
    )
    down = lax.dot_general(active, cot, TN, preferred_element_type=F32).astype(BF16)
    pre = after(pre, down)
    up = [
        lax.dot_general(normed_mid, pre[r], TN, preferred_element_type=F32).astype(BF16)
        for r in range(group)
    ]
    down = tensor_sum([down[r * local : (r + 1) * local] for r in range(group)])
    branch_w = after(branch, down, *up)
    out = lax.dot_general(mixed, branch_w, TN, preferred_element_type=F32).astype(BF16)
    up = tensor_sum(up)
    grad_mixed = after(grad_mixed, down, up, out)
    down, up = lax.psum((down, up), "dp")
    out = tensor_sum([out[r * columns : (r + 1) * columns] for r in range(group)])
    grads = attend_back(qkv, mixed, inverse, raised, grad_mixed, share, padded)
    in_planes = grads.reshape(qkv.shape)
    heads_w = [
        jnp.einsum("cte,td->ced", grads[r], normed_in, preferred_element_type=F32)
        .astype(BF16)
        .reshape(3 * columns, width)
        for r in range(group)
    ]
    heads_w = tensor_sum(heads_w)
    branch, heads_w, out = lax.optimization_barrier((branch, heads_w, out))

    steps = sum_steps([heads_w[c * columns : (c + 1) * columns] for c in range(3)] + [out])
    flying = next(steps)
    total = 2 * len(dp_bits())
    done = 0
    grad_input, parts = None, []
    half = max(share // 2, 1)
    for image in range(0, share, half):
        grad_input, *sums = input_back(
            inputs, in_planes, wqkv_all, branch, row(ln1_gain), padded, image, half, grad_input
        )
        parts.append(sums)
        if image + half < share:
            branch, flying = tie(branch, flying)
            flying = steps.send(flying)
            done += 1
    while done < total:
        if done == total - 2:
            down, up, *flying = lax.optimization_barrier((down, up) + tuple(flying))
        flying = steps.send(flying)
        done += 1
    grad_w_qkv = jnp.stack([plane.astype(F32).T for plane in flying[:3]])
    grad_w_out = flying[3].astype(F32)
    grad_w_up = up.astype(F32)
    grad_w_down = down.astype(F32)
    qkv_sums = jnp.concatenate([p[0] for p in parts])
    in_sums = jnp.concatenate([p[1] for p in parts])
    in_sum = jnp.sum(in_sums, axis=0)
    mid_sum = jnp.sum(mid_sums, axis=0)
    qkv_sum = jnp.sum(qkv_sums[:, :, 0], axis=0).reshape(group, 3, columns)
    up_sum = jnp.sum(up_sums[:, 0], axis=0).reshape(group, local)
    shards = jnp.concatenate([qkv_sum[:, 0], qkv_sum[:, 2], up_sum], axis=1)
    shard = pair_sum([shards[0]] + [swapped(shards[r], "tensor", r) for r in range(1, group)])
    whole = jnp.concatenate([in_sum[:2], mid_sum[:4]], axis=0)
    whole = pair_sum([whole] + [swapped(whole, "tensor", r) for r in range(1, group)])
    vectors = jnp.concatenate([whole.reshape(-1), shard])
    for stride, span in phases():
        vectors = pair_sum(
            [vectors] + [swapped(vectors, "dp", r * stride) for r in range(1, span)]
        )
    whole = vectors[: 6 * width].reshape(6, width)
    rest = vectors[6 * width :]
    grad_qv = rest[: 2 * columns].reshape(2, columns)
    grad_up_bias = rest[2 * columns :]
    return (
        layer_out,
        grad_input,
        whole[0],
        whole[1],
        grad_w_qkv,
        grad_qv,
        grad_w_out,
        whole[4],
        whole[2],
        whole[3],
        grad_w_up,
        grad_up_bias,
        grad_w_down,
        whole[5],
    )


def solution(mesh):
    placed = (
        P("dp", None, None),
        P(),
        P(),
        P(None, None, "tensor"),
        P(None, "tensor"),
        P("tensor", None),
        P(),
        P(),
        P(),
        P(None, "tensor"),
        P("tensor"),
        P("tensor", None),
        P(),
        P("dp", None, None),
    )
    return jax.shard_map(
        per_device,
        mesh=mesh,
        in_specs=placed,
        out_specs=(
            P(("dp", "tensor"), None, None),
            P(("dp", "tensor"), None, None),
            P(),
            P(),
            P(None, None, "tensor"),
            P(None, "tensor"),
            P("tensor", None),
            P(),
            P(),
            P(),
            P(None, "tensor"),
            P("tensor"),
            P("tensor", None),
            P(),
        ),
        check_vma=False,
    )
```
